256 devices in a mesh: band: 4 (over x_lo, core), grid: 64 (over z, y, x_hi).
Axes of the slice: x: 4 (x_hi: 2, x_lo: 2; x = x_hi * 2 + x_lo), y: 4, z: 8, core: 2. Of those that a mesh axis runs over, the one named last changes fastest.
Arguments:
- orbitals: float32 [256, 256, 8, 128], P('band', 'grid'), may hold values from -6 to 6
- potential: float32 [256, 8, 128], P('grid'), may hold values from 0 to 1.5
Outputs:
- orthonormal: float32 [256, 256, 8, 128], P('band', 'grid')
The draws below stay inside these ranges and needn't reach their ends.
All inputs are finite; a program needn't handle non-finite values.
Results may differ from the reference program's by a relative error of at most 0.000071.
Values sent between devices are 32-bit elements; how exact they have to be, the bound alone decides.
A program may use at most 64 MiB of HBM per device.

```python
import jax
import jax.numpy as jnp
from jax import lax

ORBITALS = 256
NY = 8
NZ = 128
ITERS = 2
NX = 256


def block_levels(key, extent, shards, least, top_value):
    gain, own = 1.0, jax.random.fold_in(key, 6)
    for position, shards_of in shards:
        draws = jnp.exp(jax.random.uniform(jax.random.fold_in(own, position), (shards_of,), jnp.float32, least / len(shards), top_value / len(shards)))
        gain = gain * jnp.repeat(draws, extent[position] // shards_of).reshape([-1 if axis == position else 1 for axis in range(len(extent))])
    return gain


def scatter_about(rng, dims, spread, limit, split=(), kind=jnp.bfloat16):
    values = spread * jax.random.normal(rng, dims, jnp.float32)
    if split:
        values = values * block_levels(rng, dims, split, -0.22, 0.18)
    return jnp.clip(values, -limit, limit).astype(kind)


def setup_inputs(seed: int = 0) -> dict:
    splits = jax.random.split(jax.random.key(seed), 3)
    return {
        "orbitals": scatter_about(splits[0], (ORBITALS, NX, NY, NZ), 1.0, 6.0, ((0, 4), (1, 64)), jnp.float32),
        "potential": jnp.clip(1.5 * jax.random.uniform(splits[1], (NX, NY, NZ), jnp.float32) ** block_levels(splits[1], (NX, NY, NZ), ((0, 64),), -0.2, 0.2), 0.0, 1.5),
    }


COEFS = (-205.0 / 72.0, 8.0 / 5.0, -1.0 / 5.0, 8.0 / 315.0, -1.0 / 560.0)
CENTER = 8.0
HALF = 4.0

def apply_ham(field, potential):
    lap = 3.0 * COEFS[0] * field
    for shift in range(1, 5):
        for axis in range(3):
            lap = lap + COEFS[shift] * (jnp.roll(field, shift, axis) + jnp.roll(field, -shift, axis))
    return -0.5 * lap + potential * field

def filter_one(field, potential):
    prev = field
    cur = (apply_ham(field, potential) - CENTER * field) / HALF
    for step in range(ITERS - 1):
        nxt = 2.0 * (apply_ham(cur, potential) - CENTER * cur) / HALF - prev
        prev, cur = (cur, nxt)
    return cur

def reference(orbitals, potential):
    filtered = lax.map(lambda f: filter_one(f, potential), orbitals)
    ncells = NX * NY * NZ
    flat = filtered.reshape(ORBITALS, ncells)
    margin = jnp.dot(flat.astype(jnp.float32), flat.T.astype(jnp.float32), precision=lax.Precision.HIGHEST, preferred_element_type=jnp.float32) / float(ncells)
    factor = jnp.linalg.cholesky(margin)
    ident = jnp.eye(ORBITALS, dtype=jnp.float32)
    inverse = lax.linalg.triangular_solve(factor, ident, left_side=True, lower=True)
    result = jnp.dot(inverse.astype(jnp.float32), flat.astype(jnp.float32), precision=lax.Precision.HIGHEST, preferred_element_type=jnp.float32)
    return result.reshape(ORBITALS, NX, NY, NZ)
```

```python
import functools

import jax
import jax.numpy as jnp
from jax import lax
from jax.experimental import pallas as pl
from jax.experimental.pallas import tpu as pltpu
from jax.sharding import PartitionSpec as P

MESH = pl.DeviceIdType.MESH
HIGH = lax.Precision.HIGHEST
COEFS = (-205.0 / 72.0, 8.0 / 5.0, -1.0 / 5.0, 8.0 / 315.0, -1.0 / 560.0)
CENTER = 8.0
HALF = 4.0
SCALE = -0.5 / HALF
TAPS = tuple(SCALE * c for c in COEFS)
NCELLS = 256 * 8 * 128


def nt(a, b):
    return lax.dot_general(a, b, (((1,), (1,)), ((), ())), precision=HIGH, preferred_element_type=jnp.float32)


def nn(a, b):
    return lax.dot_general(a, b, (((1,), (0,)), ((), ())), precision=HIGH, preferred_element_type=jnp.float32)


def rotate_rows(c, k):
    k = k % 8
    return c if k == 0 else jnp.concatenate([c[k:], c[:k]], axis=0)


def stencil(read, t, coef):
    c = read(t)
    total = coef * c
    for k in range(1, 5):
        s = read(t - k) + read(t + k)
        s = s + (rotate_rows(c, k) + rotate_rows(c, -k))
        s = s + (pltpu.roll(c, k, 2) + pltpu.roll(c, 128 - k, 2))
        total = total + TAPS[k] * s
    return total


def main_kernel(orb_hbm, pot_ref, mt_out, gall, x_in, stage, vbuf, ybuf, abuf, fbuf, pots,
                mt, rx, zt, rz, ty, ry, zg,
                in_sem, pot_send, pot_recv, x_send, x_recv, h_send, h_recv, a_send, a_recv,
                rx_send, rx_recv, rz_send, rz_recv, ry_send, ry_recv, zg_send, zg_recv,
                mg_send, mg_recv, ga_send, ga_recv):
    b = lax.axis_index("band")
    g = lax.axis_index("grid")
    hi = lax.rem(g, 2)
    m = g // 2
    y = lax.rem(m, 4)
    z = m // 4
    p = hi * 4 + b
    up = lax.rem(m + 1, 32)
    down = lax.rem(m + 31, 32)

    def dev(bb, gg):
        return {"band": bb, "grid": gg}

    def copy(src, dst, ssem, rsem, target):
        return pltpu.make_async_remote_copy(src_ref=src, dst_ref=dst, send_sem=ssem, recv_sem=rsem,
                                            device_id=target, device_id_type=MESH)

    def await_bytes(ref, sem):
        pltpu.make_async_copy(ref, ref, sem).wait()

    def ring(i):
        q = lax.rem(p + i, 8)
        return q, dev(lax.rem(q, 4), m * 2 + q // 4)

    def yring(i):
        yy = lax.rem(y + i, 4)
        return yy, dev(b, (z * 4 + yy) * 2 + hi)

    def zring(i):
        zz = lax.rem(z + i, 8)
        return zz, dev(b, (zz * 4 + y) * 2 + hi)

    loads = []
    for c in range(4):
        for h in range(2):
            load = pltpu.make_async_copy(orb_hbm.at[pl.ds(h * 32 + c * 8, 8)], x_in.at[h, c], in_sem.at[h, c])
            load.start()
            loads.append(load)

    other = lax.rem(g + 63 + 2 * hi, 64)
    barrier = pltpu.get_barrier_semaphore()
    peers = [ring(i)[1] for i in range(1, 8)]
    peers += [dev(b, up * 2 + hi), dev(b, down * 2 + hi), dev(b, other)]
    peers += [yring(i)[1] for i in range(1, 4)]
    peers += [zring(i)[1] for i in range(1, 8)]
    for peer in peers:
        pl.semaphore_signal(barrier, inc=1, device_id=peer, device_id_type=MESH)
    pl.semaphore_wait(barrier, len(peers))

    pots[1 + hi] = pot_ref[...]
    side = m + 2 * hi - 1
    side = lax.rem(side + 32, 32)
    pot_copies = [
        copy(pots.at[1 + hi], pots.at[1 + hi], pot_send.at[0], pot_recv, dev(b, m * 2 + 1 - hi)),
        copy(pots.at[1 + hi], pots.at[3 - 3 * hi], pot_send.at[1], pot_recv, dev(b, side * 2)),
        copy(pots.at[1 + hi], pots.at[3 - 3 * hi], pot_send.at[2], pot_recv, dev(b, side * 2 + 1)),
    ]
    for item in pot_copies:
        item.start()

    far = lax.rem(b + 2, 4)
    x_copies = []
    for c in range(4):
        for h in range(2):
            loads[2 * c + h].wait()
            for plane in range(4):
                stage[h, c, plane] = jnp.swapaxes(x_in[h, c, :, plane], 0, 1)
            item = copy(stage.at[h, c], vbuf.at[c, pl.ds(8 + 4 * hi, 4)], x_send.at[h, c], x_recv.at[c], dev(far, m * 2 + h))
            item.start()
            x_copies.append(item)

    await_bytes(pots.at[pl.ds(0, 3)], pot_recv)
    for t in range(16):
        a = pots[t // 4, t % 4] * (1.0 / HALF) + (3.0 * TAPS[0] - CENTER / HALF)
        abuf[t] = jnp.broadcast_to(a[:, None, :], (8, 8, 128))

    h_copies = []
    for c in range(4):
        await_bytes(vbuf.at[c, pl.ds(8, 8)], x_recv.at[c])
        own = vbuf.at[c, pl.ds(8, 8)]
        pair = [
            copy(own, vbuf.at[c, pl.ds(0, 8)], h_send.at[c, 0], h_recv.at[c, 0], dev(b, up * 2 + hi)),
            copy(own, vbuf.at[c, pl.ds(16, 8)], h_send.at[c, 1], h_recv.at[c, 1], dev(b, down * 2 + hi)),
        ]
        for item in pair:
            item.start()
        h_copies.append(pair)

    a_copies = []
    row = far * 8 + hi * 4
    for c in range(4):
        for item in h_copies[c]:
            item.wait_recv()

        def first(t, _):
            ybuf[t] = stencil(lambda i: vbuf[c, i], t + 4, abuf[t])
            return 0

        def second(t, _):
            fbuf[c, t] = 2.0 * stencil(lambda i: ybuf[i], t + 4, abuf[t + 4]) - vbuf[c, t + 8]
            return 0

        lax.fori_loop(0, 16, first, 0)
        lax.fori_loop(0, 8, second, 0)
        for i in range(1, 8):
            q, target = ring(i)
            item = copy(fbuf.at[c, q], gall.at[lax.rem(q, 4), row + c], a_send.at[c, i - 1], a_recv, target)
            item.start()
            a_copies.append(item)
        pltpu.make_async_copy(fbuf.at[c, p], gall.at[b, row + c], a_recv).start()
    await_bytes(gall.at[b], a_recv)

    sib = b + 1 - 2 * lax.rem(b, 2)
    to_sib = copy(gall.at[b], gall.at[b], ga_send.at[0], ga_recv.at[0], dev(sib, g))
    to_far = copy(gall.at[b], gall.at[b], ga_send.at[1], ga_recv.at[1], dev(far, g))
    relay = copy(gall.at[far], gall.at[far], ga_send.at[2], ga_recv.at[2], dev(sib, g))
    to_sib.start()

    acc = None
    for pair in range(4):
        a = jnp.concatenate([gall[b, :, 2 * pair].reshape(256, 128), gall[b, :, 2 * pair + 1].reshape(256, 128)], axis=1)
        term = nt(a, a)
        acc = term if acc is None else acc + term
    acc = acc * (1.0 / NCELLS)
    for half in range(2):
        mt[:, half * 4:half * 4 + 4] = acc[:, half * 128:half * 128 + 128].reshape(8, 4, 8, 128)

    sends = []
    for i in range(1, 8):
        q, target = ring(i)
        item = copy(mt.at[q], rx.at[i - 1], rx_send.at[i - 1], rx_recv, target)
        item.start()
        sends.append(item)
    await_bytes(rx, rx_recv)
    total = mt[p]
    for i in range(7):
        total = total + rx[i]
    zt[...] = total
    for i in range(1, 8):
        q, target = zring(i)
        item = copy(zt.at[q], rz.at[i - 1], rz_send.at[i - 1], rz_recv, target)
        item.start()
        sends.append(item)
    await_bytes(rz, rz_recv)
    tile = zt[z]
    for i in range(7):
        tile = tile + rz[i]
    ry[y] = tile
    for i in range(1, 4):
        q, target = yring(i)
        item = copy(ry.at[y], ry.at[y], ry_send.at[i - 1], ry_recv, target)
        item.start()
        sends.append(item)
    await_bytes(ty, ry_recv)
    zg[z] = ry[0] + ry[1] + ry[2] + ry[3]
    for i in range(1, 8):
        q, target = zring(i)
        item = copy(zg.at[z], zg.at[z], zg_send.at[i - 1], zg_recv, target)
        item.start()
        sends.append(item)
    await_bytes(rz, zg_recv)
    mt_out[p] = zg[...]
    for i in range(1, 8):
        q, target = ring(i)
        item = copy(zg, mt_out.at[p], mg_send.at[i - 1], mg_recv, target)
        item.start()
        sends.append(item)
    await_bytes(rx, mg_recv)

    to_far.start()
    to_far.wait_recv()
    relay.start()
    to_sib.wait_recv()
    relay.wait_recv()

    for item in pot_copies + x_copies + a_copies + sends + [to_sib, to_far, relay]:
        item.wait_send()
    for pair in h_copies:
        for item in pair:
            item.wait_send()


def inverse_factor(block):
    lane = lax.broadcasted_iota(jnp.int32, (8, 128), 1)
    sub = lax.broadcasted_iota(jnp.int32, (8, 128), 0)
    groups = [block[8 * i:8 * i + 8] for i in range(16)]
    for n in range(16):
        panel = groups[n]
        base = 8 * n
        d = [[None] * 8 for _ in range(8)]
        for j in range(8):
            column = jnp.broadcast_to(panel[:, base + j:base + j + 1], (8, 128))
            for i in range(j, 8):
                d[i][j] = jnp.broadcast_to(column[i:i + 1], (8, 128))
        inside = (lane >= base) & (lane < base + 8)
        masked = jnp.where(inside, jnp.where(lane == base + sub, 1.0, 0.0), panel)
        rows = [jnp.broadcast_to(masked[k:k + 1], (8, 128)) for k in range(8)]
        for j in range(8):
            r = lax.rsqrt(d[j][j])
            for i in range(j + 1, 8):
                d[i][j] = d[i][j] * r
            rows[j] = rows[j] * r
            for i in range(j + 1, 8):
                rows[i] = rows[i] - d[i][j] * rows[j]
                for k in range(j + 1, i + 1):
                    d[i][k] = d[i][k] - d[i][j] * d[k][j]
        out = rows[0]
        for k in range(1, 8):
            out = jnp.where(sub == k, rows[k], out)
        groups[n] = out
        for i in range(n + 1, 16):
            cur = jnp.where(inside, 0.0, groups[i])
            where = sub + 8 * i
            for j in range(8):
                cur = cur - jnp.take_along_axis(rows[j], where, axis=1) * rows[j]
            groups[i] = cur
    return jnp.concatenate([jnp.where(lane <= sub + 8 * i, groups[i], 0.0) for i in range(16)], axis=0)


def tail_kernel(mt, gall, out, w):
    b = lax.axis_index("band")

    def block(i, j):
        return mt[4 * i:4 * i + 4, 4 * j:4 * j + 4].reshape(128, 128)

    w11 = inverse_factor(block(0, 0))
    l21 = nt(block(1, 0), w11)
    w22 = inverse_factor(block(1, 1) - nt(l21, l21))
    w[0:128, 0:128] = w11
    w[0:128, 128:256] = jnp.zeros((128, 128), jnp.float32)
    w[128:256, 0:128] = -nn(w22, nn(l21, w11))
    w[128:256, 128:256] = w22
    mine = w[pl.ds(pl.multiple_of(b * 64, 64), 64), :]

    def plane(t, _):
        for pair in range(4):
            f = jnp.concatenate([gall[t, :, 2 * pair].reshape(256, 128), gall[t, :, 2 * pair + 1].reshape(256, 128)], axis=1)
            res = nn(mine, f)
            out[:, t, 2 * pair, :] = res[:, :128]
            out[:, t, 2 * pair + 1, :] = res[:, 128:]
        return 0

    lax.fori_loop(0, 4, plane, 0)


def body(orbitals, potential):
    f32 = jnp.float32
    dma = pltpu.SemaphoreType.DMA
    vmem = functools.partial(pl.BlockSpec, memory_space=pltpu.VMEM)
    mt, gall = pl.pallas_call(
        main_kernel,
        out_shape=(jax.ShapeDtypeStruct((8, 8, 8, 128), f32), jax.ShapeDtypeStruct((4, 32, 8, 8, 128), f32)),
        in_specs=[pl.BlockSpec(memory_space=pl.ANY), vmem()],
        out_specs=(vmem(), vmem()),
        scratch_shapes=[
            pltpu.VMEM((2, 4, 8, 4, 8, 128), f32),
            pltpu.VMEM((2, 4, 4, 8, 8, 128), f32),
            pltpu.VMEM((4, 24, 8, 8, 128), f32),
            pltpu.VMEM((16, 8, 8, 128), f32),
            pltpu.VMEM((16, 8, 8, 128), f32),
            pltpu.VMEM((4, 8, 8, 8, 128), f32),
            pltpu.VMEM((4, 4, 8, 128), f32),
            pltpu.VMEM((8, 8, 8, 128), f32),
            pltpu.VMEM((7, 8, 8, 128), f32),
            pltpu.VMEM((8, 8, 128), f32),
            pltpu.VMEM((7, 8, 128), f32),
            pltpu.VMEM((3, 8, 128), f32),
            pltpu.VMEM((4, 8, 128), f32),
            pltpu.VMEM((8, 8, 128), f32),
            dma((2, 4)),
            dma((3,)), dma,
            dma((2, 4)), dma((4,)),
            dma((4, 2)), dma((4, 2)),
            dma((4, 7)), dma,
            dma((7,)), dma,
            dma((7,)), dma,
            dma((3,)), dma,
            dma((7,)), dma,
            dma((7,)), dma,
            dma((3,)), dma((3,)),
        ],
        compiler_params=pltpu.CompilerParams(collective_id=0, has_side_effects=True, vmem_limit_bytes=40 * 2**20),
    )(orbitals, potential)
    return pl.pallas_call(
        tail_kernel,
        out_shape=jax.ShapeDtypeStruct(orbitals.shape, f32),
        in_specs=[vmem(), vmem()],
        out_specs=vmem(),
        scratch_shapes=[pltpu.VMEM((256, 256), f32)],
        compiler_params=pltpu.CompilerParams(vmem_limit_bytes=40 * 2**20),
    )(mt, gall)


def solution(mesh):
    return jax.shard_map(
        body,
        mesh=mesh,
        in_specs=(P("band", "grid", None, None), P("grid", None, None)),
        out_specs=P("band", "grid", None, None),
        check_vma=False,
    )
```

```python
import functools

import jax
import jax.numpy as jnp
from jax import lax
from jax.experimental import pallas as pl
from jax.experimental.pallas import tpu as pltpu
from jax.sharding import PartitionSpec as P

MESH = pl.DeviceIdType.MESH
HIGH = lax.Precision.HIGHEST
COEFS = (-205.0 / 72.0, 8.0 / 5.0, -1.0 / 5.0, 8.0 / 315.0, -1.0 / 560.0)
CENTER = 8.0
HALF = 4.0
SCALE = -0.5 / HALF
TAPS = tuple(SCALE * c for c in COEFS)
NCELLS = 256 * 8 * 128


def nt(a, b):
    return lax.dot_general(a, b, (((1,), (1,)), ((), ())), precision=HIGH, preferred_element_type=jnp.float32)


def nn(a, b):
    return lax.dot_general(a, b, (((1,), (0,)), ((), ())), precision=HIGH, preferred_element_type=jnp.float32)


def rotate_rows(c, k):
    k = k % 8
    return c if k == 0 else jnp.concatenate([c[k:], c[:k]], axis=0)


def stencil(read, t, coef):
    c = read(t)
    total = coef * c
    for k in range(1, 5):
        s = read(t - k) + read(t + k)
        s = s + (rotate_rows(c, k) + rotate_rows(c, -k))
        s = s + (pltpu.roll(c, k, 2) + pltpu.roll(c, 128 - k, 2))
        total = total + TAPS[k] * s
    return total


def main_kernel(orb_hbm, pot_hbm, w_out, gall, x_in, stage, vbuf, ybuf, abuf, fbuf, pots,
                mt, pair_in, half_sum, layer_in, zsum, mg,
                in_sem, pot_in, pot_send, pot_recv, x_send, x_recv, h_send, h_recv, a_send, a_recv,
                pair_send, pair_recv, layer_send, layer_recv, z_send, z_recv,
                spread_send, spread_recv, back_send, back_recv, ga_send, ga_recv):
    b = lax.axis_index("band")
    g = lax.axis_index("grid")
    hi = lax.rem(g, 2)
    m = g // 2
    y = lax.rem(m, 4)
    z = m // 4
    p = hi * 4 + b
    core = lax.rem(b, 2)
    chip = (y * 2 + hi) * 2 + b // 2
    up = lax.rem(m + 1, 32)
    down = lax.rem(m + 31, 32)

    def dev(bb, gg):
        return {"band": bb, "grid": gg}

    def copy(src, dst, ssem, rsem, target):
        return pltpu.make_async_remote_copy(src_ref=src, dst_ref=dst, send_sem=ssem, recv_sem=rsem,
                                            device_id=target, device_id_type=MESH)

    def await_bytes(ref, sem):
        pltpu.make_async_copy(ref, ref, sem).wait()

    def ring(i):
        q = lax.rem(p + i, 8)
        return q, dev(lax.rem(q, 4), m * 2 + q // 4)

    def layer(i):
        q = lax.rem(chip + i, 16)
        return q, dev(lax.rem(q, 2) * 2 + core, z * 8 + q // 2)

    def zring(i):
        zz = lax.rem(z + i, 8)
        return zz, dev(b, zz * 8 + y * 2 + hi)

    pot_load = pltpu.make_async_copy(pot_hbm, pots.at[1 + hi], pot_in)
    pot_load.start()
    loads = []
    for c in range(4):
        for h in range(2):
            load = pltpu.make_async_copy(orb_hbm.at[pl.ds(h * 32 + c * 8, 8)], x_in.at[h, c], in_sem.at[h, c])
            load.start()
            loads.append(load)

    other = lax.rem(g + 63 + 2 * hi, 64)
    barrier = pltpu.get_barrier_semaphore()
    peers = [ring(i)[1] for i in range(1, 8)]
    peers += [dev(b, up * 2 + hi), dev(b, down * 2 + hi), dev(b, other)]
    peers += [layer(i)[1] for i in range(1, 16)]
    peers += [zring(i)[1] for i in range(1, 8)]
    for peer in peers:
        pl.semaphore_signal(barrier, inc=1, device_id=peer, device_id_type=MESH)

    far = lax.rem(b + 2, 4)
    sib = b + 1 - 2 * core
    x_copies = []

    def turn(c):
        for h in range(2):
            loads[2 * c + h].wait()
            for plane in range(4):
                stage[h, c, plane] = jnp.swapaxes(x_in[h, c, :, plane], 0, 1)

    def send_x(c):
        for h in range(2):
            item = copy(stage.at[h, c], vbuf.at[c, pl.ds(8 + 4 * hi, 4)], x_send.at[h, c], x_recv.at[c], dev(far, m * 2 + h))
            item.start()
            x_copies.append(item)

    h_copies = {}

    def send_halo(c):
        await_bytes(vbuf.at[c, pl.ds(8, 8)], x_recv.at[c])
        own = vbuf.at[c, pl.ds(8, 8)]
        h_copies[c] = [
            copy(own, vbuf.at[c, pl.ds(0, 8)], h_send.at[c, 0], h_recv.at[c, 0], dev(b, up * 2 + hi)),
            copy(own, vbuf.at[c, pl.ds(16, 8)], h_send.at[c, 1], h_recv.at[c, 1], dev(b, down * 2 + hi)),
        ]
        for item in h_copies[c]:
            item.start()

    turn(0)
    pl.semaphore_wait(barrier, len(peers))
    send_x(0)

    pot_load.wait()
    side = lax.rem(m + 2 * hi + 31, 32)
    pot_copies = [
        copy(pots.at[1 + hi], pots.at[1 + hi], pot_send.at[0], pot_recv, dev(b, m * 2 + 1 - hi)),
        copy(pots.at[1 + hi], pots.at[3 - 3 * hi], pot_send.at[1], pot_recv, dev(b, side * 2)),
        copy(pots.at[1 + hi], pots.at[3 - 3 * hi], pot_send.at[2], pot_recv, dev(b, side * 2 + 1)),
    ]
    for item in pot_copies:
        item.start()
    turn(1)
    send_x(1)
    turn(2)
    turn(3)
    send_halo(0)
    send_x(2)
    await_bytes(pots.at[pl.ds(0, 3)], pot_recv)
    for t in range(16):
        a = pots[t // 4, t % 4] * (1.0 / HALF) + (3.0 * TAPS[0] - CENTER / HALF)
        abuf[t] = jnp.broadcast_to(a[:, None, :], (8, 8, 128))
    send_halo(1)
    send_x(3)

    a_copies = []
    row = far * 8 + hi * 4
    for c in range(4):
        for item in h_copies[c]:
            item.wait_recv()
        if c + 2 < 4:
            send_halo(c + 2)

        def first(t, _):
            ybuf[t] = stencil(lambda i: vbuf[c, i], t + 4, abuf[t])
            return 0

        def second(t, _):
            fbuf[c, t] = 2.0 * stencil(lambda i: ybuf[i], t + 4, abuf[t + 4]) - vbuf[c, t + 8]
            return 0

        lax.fori_loop(0, 16, first, 0)
        lax.fori_loop(0, 8, second, 0)
        for i in range(1, 8):
            q, target = ring(i)
            item = copy(fbuf.at[c, q], gall.at[lax.rem(q, 4), row + c], a_send.at[c, i - 1], a_recv, target)
            item.start()
            a_copies.append(item)
        pltpu.make_async_copy(fbuf.at[c, p], gall.at[b, row + c], a_recv).start()
    await_bytes(gall.at[b], a_recv)

    to_sib = copy(gall.at[b], gall.at[b], ga_send.at[0], ga_recv.at[0], dev(sib, g))
    to_far = copy(gall.at[b], gall.at[b], ga_send.at[1], ga_recv.at[1], dev(far, g))
    relay = copy(gall.at[far], gall.at[far], ga_send.at[2], ga_recv.at[2], dev(sib, g))

    acc = None
    for pair in range(4):
        a = jnp.concatenate([gall[b, :, 2 * pair].reshape(256, 128), gall[b, :, 2 * pair + 1].reshape(256, 128)], axis=1)
        term = nt(a, a)
        acc = term if acc is None else acc + term
    acc = acc * (1.0 / NCELLS)
    for half in range(2):
        mt[half] = acc[:, half * 128:half * 128 + 128].reshape(16, 2, 8, 128)

    sends = []
    item = copy(mt.at[1 - core], pair_in, pair_send, pair_recv, dev(sib, g))
    item.start()
    sends.append(item)
    item.wait_recv()
    half_sum[...] = mt[core] + pair_in[...]
    for i in range(1, 16):
        q, target = layer(i)
        item = copy(half_sum.at[q], layer_in.at[i - 1], layer_send.at[i - 1], layer_recv, target)
        item.start()
        sends.append(item)
    to_far.start()
    to_sib.start()
    await_bytes(layer_in, layer_recv)
    total = half_sum[chip]
    for i in range(15):
        total = total + layer_in[i]
    zsum[z] = total
    for i in range(1, 8):
        q, target = zring(i)
        item = copy(zsum.at[z], zsum.at[z], z_send.at[i - 1], z_recv, target)
        item.start()
        sends.append(item)
    await_bytes(zsum.at[pl.ds(0, 7)], z_recv)
    total = zsum[0]
    for i in range(1, 8):
        total = total + zsum[i]
    mg[core, chip] = total
    for i in range(1, 16):
        q, target = layer(i)
        item = copy(mg.at[core, chip], mg.at[core, chip], spread_send.at[i - 1], spread_recv, target)
        item.start()
        sends.append(item)
    await_bytes(layer_in, spread_recv)
    item = copy(mg.at[core], mg.at[core], back_send, back_recv, dev(sib, g))
    item.start()
    sends.append(item)
    item.wait_recv()

    w11 = inverse_factor(mg[0, 0:8].reshape(128, 128))
    to_far.wait_recv()
    relay.start()
    l21 = nt(mg[0, 8:16].reshape(128, 128), w11)
    w22 = inverse_factor(mg[1, 8:16].reshape(128, 128) - nt(l21, l21))
    w_out[0:128, 0:128] = w11
    w_out[0:128, 128:256] = jnp.zeros((128, 128), jnp.float32)
    w_out[128:256, 0:128] = -nn(w22, nn(l21, w11))
    w_out[128:256, 128:256] = w22
    to_sib.wait_recv()
    relay.wait_recv()

    for item in pot_copies + x_copies + a_copies + sends + [to_sib, to_far, relay]:
        item.wait_send()
    for c in range(4):
        for item in h_copies[c]:
            item.wait_send()


def inverse_factor(block):
    lane = lax.broadcasted_iota(jnp.int32, (8, 128), 1)
    sub = lax.broadcasted_iota(jnp.int32, (8, 128), 0)
    groups = [block[8 * i:8 * i + 8] for i in range(16)]
    for n in range(16):
        panel = groups[n]
        base = 8 * n
        d = [[None] * 8 for _ in range(8)]
        for j in range(8):
            column = jnp.broadcast_to(panel[:, base + j:base + j + 1], (8, 128))
            for i in range(j, 8):
                d[i][j] = jnp.broadcast_to(column[i:i + 1], (8, 128))
        inside = (lane >= base) & (lane < base + 8)
        masked = jnp.where(inside, jnp.where(lane == base + sub, 1.0, 0.0), panel)
        rows = [jnp.broadcast_to(masked[k:k + 1], (8, 128)) for k in range(8)]
        for j in range(8):
            r = lax.rsqrt(d[j][j])
            for i in range(j + 1, 8):
                d[i][j] = d[i][j] * r
            rows[j] = rows[j] * r
            for i in range(j + 1, 8):
                rows[i] = rows[i] - d[i][j] * rows[j]
                for k in range(j + 1, i + 1):
                    d[i][k] = d[i][k] - d[i][j] * d[k][j]
        out = rows[0]
        for k in range(1, 8):
            out = jnp.where(sub == k, rows[k], out)
        groups[n] = out
        for i in range(n + 1, 16):
            cur = jnp.where(inside, 0.0, groups[i])
            where = sub + 8 * i
            for j in range(8):
                cur = cur - jnp.take_along_axis(rows[j], where, axis=1) * rows[j]
            groups[i] = cur
    return jnp.concatenate([jnp.where(lane <= sub + 8 * i, groups[i], 0.0) for i in range(16)], axis=0)


def tail_kernel(w, gall, out):
    b = lax.axis_index("band")
    mine = w[pl.ds(pl.multiple_of(b * 64, 64), 64), :]

    def plane(t, _):
        for pair in range(4):
            f = jnp.concatenate([gall[t, :, 2 * pair].reshape(256, 128), gall[t, :, 2 * pair + 1].reshape(256, 128)], axis=1)
            res = nn(mine, f)
            out[:, t, 2 * pair, :] = res[:, :128]
            out[:, t, 2 * pair + 1, :] = res[:, 128:]
        return 0

    lax.fori_loop(0, 4, plane, 0)


def body(orbitals, potential):
    f32 = jnp.float32
    dma = pltpu.SemaphoreType.DMA
    vmem = functools.partial(pl.BlockSpec, memory_space=pltpu.VMEM)
    hbm = functools.partial(pl.BlockSpec, memory_space=pltpu.HBM)
    w, gall = pl.pallas_call(
        main_kernel,
        out_shape=(jax.ShapeDtypeStruct((256, 256), f32), jax.ShapeDtypeStruct((4, 32, 8, 8, 128), f32)),
        in_specs=[hbm(), hbm()],
        out_specs=(vmem(), vmem()),
        scratch_shapes=[
            pltpu.VMEM((2, 4, 8, 4, 8, 128), f32),
            pltpu.VMEM((2, 4, 4, 8, 8, 128), f32),
            pltpu.VMEM((4, 24, 8, 8, 128), f32),
            pltpu.VMEM((16, 8, 8, 128), f32),
            pltpu.VMEM((16, 8, 8, 128), f32),
            pltpu.VMEM((4, 8, 8, 8, 128), f32),
            pltpu.VMEM((4, 4, 8, 128), f32),
            pltpu.VMEM((2, 16, 2, 8, 128), f32),
            pltpu.VMEM((16, 2, 8, 128), f32),
            pltpu.VMEM((16, 2, 8, 128), f32),
            pltpu.VMEM((15, 2, 8, 128), f32),
            pltpu.VMEM((8, 2, 8, 128), f32),
            pltpu.VMEM((2, 16, 2, 8, 128), f32),
            dma((2, 4)), dma,
            dma((3,)), dma,
            dma((2, 4)), dma((4,)),
            dma((4, 2)), dma((4, 2)),
            dma((4, 7)), dma,
            dma, dma,
            dma((15,)), dma,
            dma((7,)), dma,
            dma((15,)), dma,
            dma, dma,
            dma((3,)), dma((3,)),
        ],
        compiler_params=pltpu.CompilerParams(collective_id=0, has_side_effects=True, vmem_limit_bytes=40 * 2**20),
    )(orbitals, potential)
    return pl.pallas_call(
        tail_kernel,
        out_shape=jax.ShapeDtypeStruct(orbitals.shape, f32),
        in_specs=[vmem(), vmem()],
        out_specs=vmem(),
        compiler_params=pltpu.CompilerParams(vmem_limit_bytes=40 * 2**20),
    )(w, gall)


def solution(mesh):
    return jax.shard_map(
        body,
        mesh=mesh,
        in_specs=(P("band", "grid", None, None), P("grid", None, None)),
        out_specs=P("band", "grid", None, None),
        check_vma=False,
    )
```

```python
import functools

import jax
import jax.numpy as jnp
from jax import lax
from jax.experimental import pallas as pl
from jax.experimental.pallas import tpu as pltpu
from jax.sharding import PartitionSpec as P

MESH = pl.DeviceIdType.MESH
HIGH = lax.Precision.HIGHEST
COEFS = (-205.0 / 72.0, 8.0 / 5.0, -1.0 / 5.0, 8.0 / 315.0, -1.0 / 560.0)
CENTER = 8.0
HALF = 4.0
SCALE = -0.5 / HALF
TAPS = tuple(SCALE * c for c in COEFS)
NCELLS = 256 * 8 * 128
GROUP = 4


def nt(a, b):
    return lax.dot_general(a, b, (((1,), (1,)), ((), ())), precision=HIGH, preferred_element_type=jnp.float32)


def nn(a, b):
    return lax.dot_general(a, b, (((1,), (0,)), ((), ())), precision=HIGH, preferred_element_type=jnp.float32)


def rotate_rows(c, k):
    return jnp.concatenate([c[:, k:], c[:, :k]], axis=1)


def circulant():
    i = lax.broadcasted_iota(jnp.int32, (128, 128), 0)
    j = lax.broadcasted_iota(jnp.int32, (128, 128), 1)
    apart = lax.rem(i - j + 128, 128)
    total = jnp.zeros((128, 128), jnp.float32)
    for k in range(1, 5):
        total = jnp.where((apart == k) | (apart == 128 - k), TAPS[k], total)
    return total


def stencil(read, coef, along_z):
    c = read(0)
    total = coef * c + nn(c.reshape(GROUP * 64, 128), along_z).reshape(GROUP, 8, 8, 128)
    for k in range(1, 5):
        s = read(-k) + read(k)
        s = s + (rotate_rows(c, k) + rotate_rows(c, 8 - k))
        total = total + TAPS[k] * s
    return total


def kernel(orb_hbm, pot_hbm, out_hbm, gall, x_in, stage, vbuf, ybuf, abuf, fbuf, zmat, pots, w, res,
                mt, pair_in, half_sum, layer_in, zsum, mg,
                in_sem, pot_in, pot_send, pot_recv, x_send, x_recv, h_send, h_recv, a_send, a_recv,
                pair_send, pair_recv, layer_send, layer_recv, z_send, z_recv,
                spread_send, spread_recv, back_send, back_recv, ga_send, ga_recv, out_sem):
    b = lax.axis_index("band")
    g = lax.axis_index("grid")
    hi = lax.rem(g, 2)
    m = g // 2
    y = lax.rem(m, 4)
    z = m // 4
    p = hi * 4 + b
    core = lax.rem(b, 2)
    chip = (y * 2 + hi) * 2 + b // 2
    up = lax.rem(m + 1, 32)
    down = lax.rem(m + 31, 32)

    def dev(bb, gg):
        return {"band": bb, "grid": gg}

    def copy(src, dst, ssem, rsem, target):
        return pltpu.make_async_remote_copy(src_ref=src, dst_ref=dst, send_sem=ssem, recv_sem=rsem,
                                            device_id=target, device_id_type=MESH)

    def await_bytes(ref, sem):
        pltpu.make_async_copy(ref, ref, sem).wait()

    def ring(i):
        q = lax.rem(p + i, 8)
        return q, dev(lax.rem(q, 4), m * 2 + q // 4)

    def layer(i):
        q = lax.rem(chip + i, 16)
        return q, dev(lax.rem(q, 2) * 2 + core, z * 8 + q // 2)

    def zring(i):
        zz = lax.rem(z + i, 8)
        return zz, dev(b, zz * 8 + y * 2 + hi)

    pot_load = pltpu.make_async_copy(pot_hbm, pots.at[1 + hi], pot_in)
    pot_load.start()
    loads = []
    for c in range(4):
        for h in range(2):
            load = pltpu.make_async_copy(orb_hbm.at[pl.ds(h * 32 + c * 8, 8)], x_in.at[h, c], in_sem.at[h, c])
            load.start()
            loads.append(load)

    other = lax.rem(g + 63 + 2 * hi, 64)
    barrier = pltpu.get_barrier_semaphore()
    peers = [ring(i)[1] for i in range(1, 8)]
    peers += [dev(b, up * 2 + hi), dev(b, down * 2 + hi), dev(b, other)]
    peers += [layer(i)[1] for i in range(1, 16)]
    peers += [zring(i)[1] for i in range(1, 8)]
    for peer in peers:
        pl.semaphore_signal(barrier, inc=1, device_id=peer, device_id_type=MESH)

    far = lax.rem(b + 2, 4)
    sib = b + 1 - 2 * core
    x_copies = []

    def turn(c):
        for h in range(2):
            loads[2 * c + h].wait()
            for plane in range(4):
                stage[h, c, plane] = jnp.swapaxes(x_in[h, c, :, plane], 0, 1)

    def send_x(c):
        for h in range(2):
            item = copy(stage.at[h, c], vbuf.at[c, pl.ds(8 + 4 * hi, 4)], x_send.at[h, c], x_recv.at[c], dev(far, m * 2 + h))
            item.start()
            x_copies.append(item)

    h_copies = {}

    def send_halo(c):
        await_bytes(vbuf.at[c, pl.ds(8, 8)], x_recv.at[c])
        own = vbuf.at[c, pl.ds(8, 8)]
        h_copies[c] = [
            copy(own, vbuf.at[c, pl.ds(0, 8)], h_send.at[c, 0], h_recv.at[c, 0], dev(b, up * 2 + hi)),
            copy(own, vbuf.at[c, pl.ds(16, 8)], h_send.at[c, 1], h_recv.at[c, 1], dev(b, down * 2 + hi)),
        ]
        for item in h_copies[c]:
            item.start()

    turn(0)
    zmat[...] = circulant()
    pl.semaphore_wait(barrier, len(peers))
    send_x(0)

    pot_load.wait()
    side = lax.rem(m + 2 * hi + 31, 32)
    pot_copies = [
        copy(pots.at[1 + hi], pots.at[1 + hi], pot_send.at[0], pot_recv, dev(b, m * 2 + 1 - hi)),
        copy(pots.at[1 + hi], pots.at[3 - 3 * hi], pot_send.at[1], pot_recv, dev(b, side * 2)),
        copy(pots.at[1 + hi], pots.at[3 - 3 * hi], pot_send.at[2], pot_recv, dev(b, side * 2 + 1)),
    ]
    for item in pot_copies:
        item.start()
    turn(1)
    send_x(1)
    turn(2)
    turn(3)
    send_halo(0)
    send_x(2)
    await_bytes(pots.at[pl.ds(0, 3)], pot_recv)
    for t in range(16):
        a = pots[t // 4, t % 4] * (1.0 / HALF) + (3.0 * TAPS[0] - CENTER / HALF)
        abuf[t] = jnp.broadcast_to(a[:, None, :], (8, 8, 128))
    send_halo(1)
    send_x(3)

    to_sib, to_far, relay = [], [], []

    def send_plane(c):
        to_far.append(copy(gall.at[b, c], gall.at[b, c], ga_send.at[1, c], ga_recv.at[1, c], dev(far, g)))
        to_sib.append(copy(gall.at[b, c], gall.at[b, c], ga_send.at[0, c], ga_recv.at[0, c], dev(sib, g)))
        to_far[c].start()
        to_sib[c].start()

    def send_relay(c):
        to_far[c].wait_recv()
        relay.append(copy(gall.at[far, c], gall.at[far, c], ga_send.at[2, c], ga_recv.at[2, c], dev(sib, g)))
        relay[c].start()

    a_copies = []
    row = far * 2 + hi
    for c in range(4):
        for item in h_copies[c]:
            item.wait_recv()
        if c + 2 < 4:
            send_halo(c + 2)

        def first(i, _):
            t = i * GROUP
            ybuf[pl.ds(t, GROUP)] = stencil(lambda k: vbuf[c, pl.ds(t + 4 + k, GROUP)], abuf[pl.ds(t, GROUP)], zmat[...])
            return 0

        def second(i, _):
            t = i * GROUP
            step = stencil(lambda k: ybuf[pl.ds(t + 4 + k, GROUP)], abuf[pl.ds(t + 4, GROUP)], zmat[...])
            fbuf[c, pl.ds(t, GROUP)] = 2.0 * step - vbuf[c, pl.ds(t + 8, GROUP)]
            return 0

        lax.fori_loop(0, 16 // GROUP, first, 0, unroll=2)
        lax.fori_loop(0, 8 // GROUP, second, 0, unroll=2)
        for i in range(1, 8):
            q, target = ring(i)
            item = copy(fbuf.at[c, q], gall.at[lax.rem(q, 4), c, row], a_send.at[c, i - 1], a_recv.at[c], target)
            item.start()
            a_copies.append(item)
        pltpu.make_async_copy(fbuf.at[c, p], gall.at[b, c, row], a_recv.at[c]).start()
        if c >= 1:
            await_bytes(gall.at[b, c - 1], a_recv.at[c - 1])
        if c in (1, 2):
            send_plane(c - 1)
    send_relay(0)
    await_bytes(gall.at[b, 3], a_recv.at[3])

    def orbitals_of(t, pair):
        return jnp.concatenate([
            jnp.concatenate([gall[t, c, slot, row] for slot in range(8) for c in range(4)], axis=0)
            for row in (2 * pair, 2 * pair + 1)], axis=1)

    acc = None
    for pair in range(4):
        a = orbitals_of(b, pair)
        term = nt(a, a)
        acc = term if acc is None else acc + term
    acc = acc * (1.0 / NCELLS)
    for half in range(2):
        mt[half] = acc[:, half * 128:half * 128 + 128].reshape(16, 2, 8, 128)

    sends = []
    item = copy(mt.at[1 - core], pair_in, pair_send, pair_recv, dev(sib, g))
    item.start()
    sends.append(item)
    item.wait_recv()
    half_sum[...] = mt[core] + pair_in[...]
    for i in range(1, 16):
        q, target = layer(i)
        item = copy(half_sum.at[q], layer_in.at[i - 1], layer_send.at[i - 1], layer_recv, target)
        item.start()
        sends.append(item)
    send_plane(2)
    send_plane(3)
    await_bytes(layer_in, layer_recv)
    total = half_sum[chip]
    for i in range(15):
        total = total + layer_in[i]
    zsum[z] = total
    for i in range(1, 8):
        q, target = zring(i)
        item = copy(zsum.at[z], zsum.at[z], z_send.at[i - 1], z_recv, target)
        item.start()
        sends.append(item)
    await_bytes(zsum.at[pl.ds(0, 7)], z_recv)
    total = zsum[0]
    for i in range(1, 8):
        total = total + zsum[i]
    mg[core, chip] = total
    for i in range(1, 16):
        q, target = layer(i)
        item = copy(mg.at[core, chip], mg.at[core, chip], spread_send.at[i - 1], spread_recv, target)
        item.start()
        sends.append(item)
    await_bytes(layer_in, spread_recv)
    item = copy(mg.at[core], mg.at[core], back_send, back_recv, dev(sib, g))
    item.start()
    sends.append(item)
    item.wait_recv()

    send_relay(1)
    w11 = inverse_factor(mg[0, 0:8].reshape(128, 128))
    send_relay(2)
    send_relay(3)
    l21 = nt(mg[0, 8:16].reshape(128, 128), w11)
    w22 = inverse_factor(mg[1, 8:16].reshape(128, 128) - nt(l21, l21))
    w[0:128, 0:128] = w11
    w[0:128, 128:256] = jnp.zeros((128, 128), jnp.float32)
    w[128:256, 0:128] = -nn(w22, nn(l21, w11))
    w[128:256, 128:256] = w22

    mine = w[pl.ds(pl.multiple_of(b * 64, 64), 64), :]
    outs = []
    for n, t in enumerate((b, sib, far, lax.rem(sib + 2, 4))):
        for c in range(4):
            if n == 1:
                to_sib[c].wait_recv()
            if n == 3:
                relay[c].wait_recv()
        for pair in range(4):
            block = nn(mine, orbitals_of(t, pair))
            res[t, :, 2 * pair, :] = block[:, :128]
            res[t, :, 2 * pair + 1, :] = block[:, 128:]
        item = pltpu.make_async_copy(res.at[t], out_hbm.at[:, t], out_sem.at[n])
        item.start()
        outs.append(item)

    for item in pot_copies + x_copies + a_copies + sends + to_sib + to_far + relay:
        item.wait_send()
    for c in range(4):
        for item in h_copies[c]:
            item.wait_send()
    for item in outs:
        item.wait()


def inverse_factor(block):
    lane = lax.broadcasted_iota(jnp.int32, (8, 128), 1)
    sub = lax.broadcasted_iota(jnp.int32, (8, 128), 0)
    groups = [block[8 * i:8 * i + 8] for i in range(16)]
    for n in range(16):
        panel = groups[n]
        base = 8 * n
        d = [[None] * 8 for _ in range(8)]
        for j in range(8):
            column = jnp.broadcast_to(panel[:, base + j:base + j + 1], (8, 128))
            for i in range(j, 8):
                d[i][j] = jnp.broadcast_to(column[i:i + 1], (8, 128))
        inside = (lane >= base) & (lane < base + 8)
        masked = jnp.where(inside, jnp.where(lane == base + sub, 1.0, 0.0), panel)
        rows = [jnp.broadcast_to(masked[k:k + 1], (8, 128)) for k in range(8)]
        for j in range(8):
            r = lax.rsqrt(d[j][j])
            for i in range(j + 1, 8):
                d[i][j] = d[i][j] * r
            rows[j] = rows[j] * r
            for i in range(j + 1, 8):
                rows[i] = rows[i] - d[i][j] * rows[j]
                for k in range(j + 1, i + 1):
                    d[i][k] = d[i][k] - d[i][j] * d[k][j]
        out = rows[0]
        for k in range(1, 8):
            out = jnp.where(sub == k, rows[k], out)
        groups[n] = out
        for i in range(n + 1, 16):
            cur = jnp.where(inside, 0.0, groups[i])
            where = sub + 8 * i
            for j in range(8):
                cur = cur - jnp.take_along_axis(rows[j], where, axis=1) * rows[j]
            groups[i] = cur
    return jnp.concatenate([jnp.where(lane <= sub + 8 * i, groups[i], 0.0) for i in range(16)], axis=0)


def body(orbitals, potential):
    f32 = jnp.float32
    dma = pltpu.SemaphoreType.DMA
    hbm = functools.partial(pl.BlockSpec, memory_space=pl.ANY)
    return pl.pallas_call(
        kernel,
        out_shape=jax.ShapeDtypeStruct(orbitals.shape, f32),
        in_specs=[hbm(), hbm()],
        out_specs=hbm(),
        scratch_shapes=[
            pltpu.VMEM((4, 4, 8, 8, 8, 128), f32),
            pltpu.VMEM((2, 4, 8, 4, 8, 128), f32),
            pltpu.VMEM((2, 4, 4, 8, 8, 128), f32),
            pltpu.VMEM((4, 24, 8, 8, 128), f32),
            pltpu.VMEM((16, 8, 8, 128), f32),
            pltpu.VMEM((16, 8, 8, 128), f32),
            pltpu.VMEM((4, 8, 8, 8, 128), f32),
            pltpu.VMEM((128, 128), f32),
            pltpu.VMEM((4, 4, 8, 128), f32),
            pltpu.VMEM((256, 256), f32),
            pltpu.VMEM((4, 64, 8, 128), f32),
            pltpu.VMEM((2, 16, 2, 8, 128), f32),
            pltpu.VMEM((16, 2, 8, 128), f32),
            pltpu.VMEM((16, 2, 8, 128), f32),
            pltpu.VMEM((15, 2, 8, 128), f32),
            pltpu.VMEM((8, 2, 8, 128), f32),
            pltpu.VMEM((2, 16, 2, 8, 128), f32),
            dma((2, 4)), dma,
            dma((3,)), dma,
            dma((2, 4)), dma((4,)),
            dma((4, 2)), dma((4, 2)),
            dma((4, 7)), dma((4,)),
            dma, dma,
            dma((15,)), dma,
            dma((7,)), dma,
            dma((15,)), dma,
            dma, dma,
            dma((3, 4)), dma((3, 4)), dma((4,)),
        ],
        compiler_params=pltpu.CompilerParams(collective_id=0, has_side_effects=True, vmem_limit_bytes=60 * 2**20),
    )(orbitals, potential)


def solution(mesh):
    return jax.shard_map(
        body,
        mesh=mesh,
        in_specs=(P("band", "grid", None, None), P("grid", None, None)),
        out_specs=P("band", "grid", None, None),
        check_vma=False,
    )
```

```python
import functools

import jax
import jax.numpy as jnp
from jax import lax
from jax.experimental import pallas as pl
from jax.experimental.pallas import tpu as pltpu
from jax.sharding import PartitionSpec as P

MESH = pl.DeviceIdType.MESH
HIGH = lax.Precision.HIGHEST
COEFS = (-205.0 / 72.0, 8.0 / 5.0, -1.0 / 5.0, 8.0 / 315.0, -1.0 / 560.0)
CENTER = 8.0
HALF = 4.0
SCALE = -0.5 / HALF
TAPS = tuple(SCALE * c for c in COEFS)
NCELLS = 256 * 8 * 128
GROUP = 4


def nt(a, b):
    return lax.dot_general(a, b, (((1,), (1,)), ((), ())), precision=HIGH, preferred_element_type=jnp.float32)


def nn(a, b):
    return lax.dot_general(a, b, (((1,), (0,)), ((), ())), precision=HIGH, preferred_element_type=jnp.float32)


def rotate_rows(c, k):
    return jnp.concatenate([c[:, k:], c[:, :k]], axis=1)


def circulant():
    i = lax.broadcasted_iota(jnp.int32, (128, 128), 0)
    j = lax.broadcasted_iota(jnp.int32, (128, 128), 1)
    apart = lax.rem(i - j + 128, 128)
    total = jnp.zeros((128, 128), jnp.float32)
    for k in range(1, 5):
        total = jnp.where((apart == k) | (apart == 128 - k), TAPS[k], total)
    return total


def stencil(read, coef, along_z):
    c = read(0)
    total = coef * c + nn(c.reshape(GROUP * 64, 128), along_z).reshape(GROUP, 8, 8, 128)
    for k in range(1, 5):
        s = read(-k) + read(k)
        s = s + (rotate_rows(c, k) + rotate_rows(c, 8 - k))
        total = total + TAPS[k] * s
    return total


def orbitals_of(gall, t, pair):
    return jnp.concatenate([
        jnp.concatenate([gall[t, c, slot, row] for slot in range(8) for c in range(4)], axis=0)
        for row in (2 * pair, 2 * pair + 1)], axis=1)


def main_kernel(orb_hbm, pot_hbm, w, gall, x_in, stage, vbuf, ybuf, abuf, fbuf, zmat, pots,
                mt, pair_in, half_sum, layer_in, zsum, mg,
                in_sem, pot_in, pot_send, pot_recv, x_send, x_recv, h_send, h_recv, a_send, a_recv,
                pair_send, pair_recv, layer_send, layer_recv, z_send, z_recv,
                spread_send, spread_recv, back_send, back_recv, ga_send, ga_recv):
    b = lax.axis_index("band")
    g = lax.axis_index("grid")
    hi = lax.rem(g, 2)
    m = g // 2
    y = lax.rem(m, 4)
    z = m // 4
    p = hi * 4 + b
    core = lax.rem(b, 2)
    chip = (y * 2 + hi) * 2 + b // 2
    up = lax.rem(m + 1, 32)
    down = lax.rem(m + 31, 32)

    def dev(bb, gg):
        return {"band": bb, "grid": gg}

    def copy(src, dst, ssem, rsem, target):
        return pltpu.make_async_remote_copy(src_ref=src, dst_ref=dst, send_sem=ssem, recv_sem=rsem,
                                            device_id=target, device_id_type=MESH)

    def await_bytes(ref, sem):
        pltpu.make_async_copy(ref, ref, sem).wait()

    def ring(i):
        q = lax.rem(p + i, 8)
        return q, dev(lax.rem(q, 4), m * 2 + q // 4)

    def layer(i):
        q = lax.rem(chip + i, 16)
        return q, dev(lax.rem(q, 2) * 2 + core, z * 8 + q // 2)

    def zring(i):
        zz = lax.rem(z + i, 8)
        return zz, dev(b, zz * 8 + y * 2 + hi)

    pot_load = pltpu.make_async_copy(pot_hbm, pots.at[1 + hi], pot_in)
    pot_load.start()
    loads = []
    for c in range(4):
        for h in range(2):
            load = pltpu.make_async_copy(orb_hbm.at[pl.ds(h * 32 + c * 8, 8)], x_in.at[h, c], in_sem.at[h, c])
            load.start()
            loads.append(load)

    other = lax.rem(g + 63 + 2 * hi, 64)
    barrier = pltpu.get_barrier_semaphore()
    peers = [ring(i)[1] for i in range(1, 8)]
    peers += [dev(b, up * 2 + hi), dev(b, down * 2 + hi), dev(b, other)]
    peers += [layer(i)[1] for i in range(1, 16)]
    peers += [zring(i)[1] for i in range(1, 8)]
    for peer in peers:
        pl.semaphore_signal(barrier, inc=1, device_id=peer, device_id_type=MESH)

    far = lax.rem(b + 2, 4)
    sib = b + 1 - 2 * core
    x_copies = []

    def turn(c):
        for h in range(2):
            loads[2 * c + h].wait()
            for plane in range(4):
                stage[h, c, plane] = jnp.swapaxes(x_in[h, c, :, plane], 0, 1)

    def send_x(c):
        for h in range(2):
            item = copy(stage.at[h, c], vbuf.at[c, pl.ds(8 + 4 * hi, 4)], x_send.at[h, c], x_recv.at[c], dev(far, m * 2 + h))
            item.start()
            x_copies.append(item)

    h_copies = {}

    def send_halo(c):
        await_bytes(vbuf.at[c, pl.ds(8, 8)], x_recv.at[c])
        own = vbuf.at[c, pl.ds(8, 8)]
        h_copies[c] = [
            copy(own, vbuf.at[c, pl.ds(0, 8)], h_send.at[c, 0], h_recv.at[c, 0], dev(b, up * 2 + hi)),
            copy(own, vbuf.at[c, pl.ds(16, 8)], h_send.at[c, 1], h_recv.at[c, 1], dev(b, down * 2 + hi)),
        ]
        for item in h_copies[c]:
            item.start()

    turn(0)
    zmat[...] = circulant()
    pl.semaphore_wait(barrier, len(peers))
    send_x(0)

    pot_load.wait()
    side = lax.rem(m + 2 * hi + 31, 32)
    pot_copies = [
        copy(pots.at[1 + hi], pots.at[1 + hi], pot_send.at[0], pot_recv, dev(b, m * 2 + 1 - hi)),
        copy(pots.at[1 + hi], pots.at[3 - 3 * hi], pot_send.at[1], pot_recv, dev(b, side * 2)),
        copy(pots.at[1 + hi], pots.at[3 - 3 * hi], pot_send.at[2], pot_recv, dev(b, side * 2 + 1)),
    ]
    for item in pot_copies:
        item.start()
    turn(1)
    send_x(1)
    turn(2)
    turn(3)
    send_halo(0)
    send_x(2)
    await_bytes(pots.at[pl.ds(0, 3)], pot_recv)
    for t in range(16):
        a = pots[t // 4, t % 4] * (1.0 / HALF) + (3.0 * TAPS[0] - CENTER / HALF)
        abuf[t] = jnp.broadcast_to(a[:, None, :], (8, 8, 128))
    send_halo(1)
    send_x(3)

    to_sib, to_far, relay = [], [], []

    def send_plane(c):
        to_far.append(copy(gall.at[b, c], gall.at[b, c], ga_send.at[1, c], ga_recv.at[1, c], dev(far, g)))
        to_sib.append(copy(gall.at[b, c], gall.at[b, c], ga_send.at[0, c], ga_recv.at[0, c], dev(sib, g)))
        to_far[c].start()
        to_sib[c].start()

    def send_relay(c):
        to_far[c].wait_recv()
        relay.append(copy(gall.at[far, c], gall.at[far, c], ga_send.at[2, c], ga_recv.at[2, c], dev(sib, g)))
        relay[c].start()

    a_copies = []
    row = far * 2 + hi
    for c in range(4):
        for item in h_copies[c]:
            item.wait_recv()
        if c + 2 < 4:
            send_halo(c + 2)

        def first(i, _):
            t = i * GROUP
            ybuf[pl.ds(t, GROUP)] = stencil(lambda k: vbuf[c, pl.ds(t + 4 + k, GROUP)], abuf[pl.ds(t, GROUP)], zmat[...])
            return 0

        def second(i, _):
            t = i * GROUP
            step = stencil(lambda k: ybuf[pl.ds(t + 4 + k, GROUP)], abuf[pl.ds(t + 4, GROUP)], zmat[...])
            fbuf[c, pl.ds(t, GROUP)] = 2.0 * step - vbuf[c, pl.ds(t + 8, GROUP)]
            return 0

        lax.fori_loop(0, 16 // GROUP, first, 0, unroll=2)
        lax.fori_loop(0, 8 // GROUP, second, 0, unroll=2)
        for i in range(1, 8):
            q, target = ring(i)
            item = copy(fbuf.at[c, q], gall.at[lax.rem(q, 4), c, row], a_send.at[c, i - 1], a_recv.at[c], target)
            item.start()
            a_copies.append(item)
        pltpu.make_async_copy(fbuf.at[c, p], gall.at[b, c, row], a_recv.at[c]).start()
        if c >= 1:
            await_bytes(gall.at[b, c - 1], a_recv.at[c - 1])
    await_bytes(gall.at[b, 3], a_recv.at[3])

    acc = None
    for pair in range(4):
        a = orbitals_of(gall, b, pair)
        term = nt(a, a)
        acc = term if acc is None else acc + term
    acc = acc * (1.0 / NCELLS)
    for half in range(2):
        mt[half] = acc[:, half * 128:half * 128 + 128].reshape(16, 2, 8, 128)

    sends = []
    item = copy(mt.at[1 - core], pair_in, pair_send, pair_recv, dev(sib, g))
    item.start()
    sends.append(item)
    item.wait_recv()
    half_sum[...] = mt[core] + pair_in[...]
    for i in range(1, 16):
        q, target = layer(i)
        item = copy(half_sum.at[q], layer_in.at[i - 1], layer_send.at[i - 1], layer_recv, target)
        item.start()
        sends.append(item)
    send_plane(0)
    send_plane(1)
    await_bytes(layer_in, layer_recv)
    total = half_sum[chip]
    for i in range(15):
        total = total + layer_in[i]
    zsum[z] = total
    for i in range(1, 8):
        q, target = zring(i)
        item = copy(zsum.at[z], zsum.at[z], z_send.at[i - 1], z_recv, target)
        item.start()
        sends.append(item)
    await_bytes(zsum.at[pl.ds(0, 7)], z_recv)
    total = zsum[0]
    for i in range(1, 8):
        total = total + zsum[i]
    mg[core, chip] = total
    for i in range(1, 16):
        q, target = layer(i)
        item = copy(mg.at[core, chip], mg.at[core, chip], spread_send.at[i - 1], spread_recv, target)
        item.start()
        sends.append(item)
    send_plane(2)
    send_plane(3)
    await_bytes(layer_in, spread_recv)
    item = copy(mg.at[core], mg.at[core], back_send, back_recv, dev(sib, g))
    item.start()
    sends.append(item)
    item.wait_recv()

    send_relay(0)
    send_relay(1)
    w11 = inverse_factor(mg[0, 0:8].reshape(128, 128))
    send_relay(2)
    l21 = nt(mg[0, 8:16].reshape(128, 128), w11)
    w22 = inverse_factor(mg[1, 8:16].reshape(128, 128) - nt(l21, l21))
    w[0:128, 0:128] = w11
    w[0:128, 128:256] = jnp.zeros((128, 128), jnp.float32)
    w[128:256, 0:128] = -nn(w22, nn(l21, w11))
    w[128:256, 128:256] = w22
    send_relay(3)

    for c in range(4):
        to_sib[c].wait_recv()
        relay[c].wait_recv()
    for item in pot_copies + x_copies + a_copies + sends + to_sib + to_far + relay:
        item.wait_send()
    for c in range(4):
        for item in h_copies[c]:
            item.wait_send()


def inverse_factor(block):
    lane = lax.broadcasted_iota(jnp.int32, (8, 128), 1)
    sub = lax.broadcasted_iota(jnp.int32, (8, 128), 0)
    groups = [block[8 * i:8 * i + 8] for i in range(16)]
    for n in range(16):
        panel = groups[n]
        base = 8 * n
        d = [[None] * 8 for _ in range(8)]
        for j in range(8):
            column = jnp.broadcast_to(panel[:, base + j:base + j + 1], (8, 128))
            for i in range(j, 8):
                d[i][j] = jnp.broadcast_to(column[i:i + 1], (8, 128))
        inside = (lane >= base) & (lane < base + 8)
        masked = jnp.where(inside, jnp.where(lane == base + sub, 1.0, 0.0), panel)
        rows = [jnp.broadcast_to(masked[k:k + 1], (8, 128)) for k in range(8)]
        for j in range(8):
            r = lax.rsqrt(d[j][j])
            for i in range(j + 1, 8):
                d[i][j] = d[i][j] * r
            rows[j] = rows[j] * r
            for i in range(j + 1, 8):
                rows[i] = rows[i] - d[i][j] * rows[j]
                for k in range(j + 1, i + 1):
                    d[i][k] = d[i][k] - d[i][j] * d[k][j]
        out = rows[0]
        for k in range(1, 8):
            out = jnp.where(sub == k, rows[k], out)
        groups[n] = out
        for i in range(n + 1, 16):
            cur = jnp.where(inside, 0.0, groups[i])
            where = sub + 8 * i
            for j in range(8):
                cur = cur - jnp.take_along_axis(rows[j], where, axis=1) * rows[j]
            groups[i] = cur
    return jnp.concatenate([jnp.where(lane <= sub + 8 * i, groups[i], 0.0) for i in range(16)], axis=0)


def product_kernel(w, gall, out_hbm, res, out_sem):
    b = lax.axis_index("band")
    mine = w[pl.ds(pl.multiple_of(b * 64, 64), 64), :]
    outs = []
    for t in range(4):
        for pair in range(4):
            block = nn(mine, orbitals_of(gall, t, pair))
            res[t, :, 2 * pair, :] = block[:, :128]
            res[t, :, 2 * pair + 1, :] = block[:, 128:]
        item = pltpu.make_async_copy(res.at[t], out_hbm.at[:, t], out_sem.at[t])
        item.start()
        outs.append(item)
    for item in outs:
        item.wait()


def body(orbitals, potential):
    f32 = jnp.float32
    dma = pltpu.SemaphoreType.DMA
    anywhere = functools.partial(pl.BlockSpec, memory_space=pl.ANY)
    vmem = functools.partial(pl.BlockSpec, memory_space=pltpu.VMEM)
    orbitals = pltpu.with_memory_space_constraint(orbitals, pltpu.HBM)
    potential = pltpu.with_memory_space_constraint(potential, pltpu.HBM)
    w, gall = pl.pallas_call(
        main_kernel,
        out_shape=(jax.ShapeDtypeStruct((256, 256), f32), jax.ShapeDtypeStruct((4, 4, 8, 8, 8, 128), f32)),
        in_specs=[anywhere(), anywhere()],
        out_specs=(vmem(), vmem()),
        scratch_shapes=[
            pltpu.VMEM((2, 4, 8, 4, 8, 128), f32),
            pltpu.VMEM((2, 4, 4, 8, 8, 128), f32),
            pltpu.VMEM((4, 24, 8, 8, 128), f32),
            pltpu.VMEM((16, 8, 8, 128), f32),
            pltpu.VMEM((16, 8, 8, 128), f32),
            pltpu.VMEM((4, 8, 8, 8, 128), f32),
            pltpu.VMEM((128, 128), f32),
            pltpu.VMEM((4, 4, 8, 128), f32),
            pltpu.VMEM((2, 16, 2, 8, 128), f32),
            pltpu.VMEM((16, 2, 8, 128), f32),
            pltpu.VMEM((16, 2, 8, 128), f32),
            pltpu.VMEM((15, 2, 8, 128), f32),
            pltpu.VMEM((8, 2, 8, 128), f32),
            pltpu.VMEM((2, 16, 2, 8, 128), f32),
            dma((2, 4)), dma,
            dma((3,)), dma,
            dma((2, 4)), dma((4,)),
            dma((4, 2)), dma((4, 2)),
            dma((4, 7)), dma((4,)),
            dma, dma,
            dma((15,)), dma,
            dma((7,)), dma,
            dma((15,)), dma,
            dma, dma,
            dma((3, 4)), dma((3, 4)),
        ],
        compiler_params=pltpu.CompilerParams(collective_id=0, has_side_effects=True, vmem_limit_bytes=40 * 2**20),
    )(orbitals, potential)
    return pl.pallas_call(
        product_kernel,
        out_shape=jax.ShapeDtypeStruct(orbitals.shape, f32),
        in_specs=[vmem(), vmem()],
        out_specs=anywhere(),
        scratch_shapes=[pltpu.VMEM((4, 64, 8, 128), f32), dma((4,))],
        compiler_params=pltpu.CompilerParams(vmem_limit_bytes=40 * 2**20),
    )(w, gall)


def solution(mesh):
    return jax.shard_map(
        body,
        mesh=mesh,
        in_specs=(P("band", "grid", None, None), P("grid", None, None)),
        out_specs=P("band", "grid", None, None),
        check_vma=False,
    )
```

```python
import functools

import jax
import jax.numpy as jnp
from jax import lax
from jax.experimental import pallas as pl
from jax.experimental.pallas import tpu as pltpu
from jax.sharding import PartitionSpec as P

MESH = pl.DeviceIdType.MESH
HIGH = lax.Precision.HIGHEST
COEFS = (-205.0 / 72.0, 8.0 / 5.0, -1.0 / 5.0, 8.0 / 315.0, -1.0 / 560.0)
CENTER = 8.0
HALF = 4.0
SCALE = -0.5 / HALF
TAPS = tuple(SCALE * c for c in COEFS)
NCELLS = 256 * 8 * 128
GROUP = 4

SPLIT = (0, 1, 1, 4)


def nt(a, b):
    return lax.dot_general(a, b, (((1,), (1,)), ((), ())), precision=HIGH, preferred_element_type=jnp.float32)


def nn(a, b):
    return lax.dot_general(a, b, (((1,), (0,)), ((), ())), precision=HIGH, preferred_element_type=jnp.float32)


def rotate_rows(c, k):
    return jnp.concatenate([c[:, k:], c[:, :k]], axis=1)


def circulant():
    i = lax.broadcasted_iota(jnp.int32, (128, 128), 0)
    j = lax.broadcasted_iota(jnp.int32, (128, 128), 1)
    apart = lax.rem(i - j + 128, 128)
    total = jnp.zeros((128, 128), jnp.float32)
    for k in range(1, 5):
        total = jnp.where((apart == k) | (apart == 128 - k), TAPS[k], total)
    return total


def stencil(read, coef, along_z):
    c = read(0)
    total = coef * c + nn(c.reshape(GROUP * 64, 128), along_z).reshape(GROUP, 8, 8, 128)
    for k in range(1, 5):
        s = read(-k) + read(k)
        s = s + (rotate_rows(c, k) + rotate_rows(c, 8 - k))
        total = total + TAPS[k] * s
    return total


def orbitals_of(gall, t, pair):
    return jnp.concatenate([
        jnp.concatenate([gall[t, c, slot, row] for slot in range(8) for c in range(4)], axis=0)
        for row in (2 * pair, 2 * pair + 1)], axis=1)


def main_kernel(orb_hbm, pot_hbm, w, gall, x_in, stage, vbuf, ybuf, abuf, fbuf, zmat, pots,
                mt, pair_in, half_sum, layer_in, zsum, mg,
                in_sem, pot_in, pot_send, pot_recv, x_send, x_recv, first_send, first_recv, first_out, h_send, h_recv, a_send, a_recv,
                pair_send, pair_recv, layer_send, layer_recv, z_send, z_recv,
                spread_send, spread_recv, back_send, back_recv, ga_send, ga_recv):
    b = lax.axis_index("band")
    g = lax.axis_index("grid")
    hi = lax.rem(g, 2)
    m = g // 2
    y = lax.rem(m, 4)
    z = m // 4
    p = hi * 4 + b
    core = lax.rem(b, 2)
    chip = (y * 2 + hi) * 2 + b // 2
    up = lax.rem(m + 1, 32)
    down = lax.rem(m + 31, 32)

    def dev(bb, gg):
        return {"band": bb, "grid": gg}

    def copy(src, dst, ssem, rsem, target):
        return pltpu.make_async_remote_copy(src_ref=src, dst_ref=dst, send_sem=ssem, recv_sem=rsem,
                                            device_id=target, device_id_type=MESH)

    def await_bytes(ref, sem):
        pltpu.make_async_copy(ref, ref, sem).wait()

    def ring(i):
        q = lax.rem(p + i, 8)
        return q, dev(lax.rem(q, 4), m * 2 + q // 4)

    def layer(i):
        q = lax.rem(chip + i, 16)
        return q, dev(lax.rem(q, 2) * 2 + core, z * 8 + q // 2)

    def zring(i):
        zz = lax.rem(z + i, 8)
        return zz, dev(b, zz * 8 + y * 2 + hi)

    other = lax.rem(g + 63 + 2 * hi, 64)
    barrier = pltpu.get_barrier_semaphore()
    peers = [zring(i)[1] for i in (4, 3, 5, 2, 6, 1, 7)]
    peers += [layer(i)[1] for i in (10, 9, 11, 6, 14, 8, 2, 7, 13, 5, 3, 1, 4, 12, 15)]
    peers += [ring(i)[1] for i in range(1, 8)]
    peers += [dev(b, up * 2 + hi), dev(b, down * 2 + hi), dev(b, other)]
    for peer in peers:
        pl.semaphore_signal(barrier, inc=1, device_id=peer, device_id_type=MESH)

    pot_load = pltpu.make_async_copy(pot_hbm, pots.at[1 + hi], pot_in)
    pot_load.start()
    loads = []
    for c in range(4):
        for h in range(2):
            load = pltpu.make_async_copy(orb_hbm.at[pl.ds(h * 32 + c * 8, 8)], x_in.at[h, c], in_sem.at[h, c])
            load.start()
            loads.append(load)

    far = lax.rem(b + 2, 4)
    sib = b + 1 - 2 * core
    x_copies = []

    def turn(c):
        for h in range(2):
            loads[2 * c + h].wait()
            for plane in range(4):
                stage[h, c, plane] = jnp.swapaxes(x_in[h, c, :, plane], 0, 1)

    def send_x(c):
        for h in range(2):
            if c == 0:
                for t in range(4):
                    item = copy(stage.at[h, 0, t], vbuf.at[0, 8 + 4 * hi + t], first_send.at[h, t], first_recv.at[t], dev(far, m * 2 + h))
                    item.start()
                    x_copies.append(item)
                continue
            item = copy(stage.at[h, c], vbuf.at[c, pl.ds(8 + 4 * hi, 4)], x_send.at[h, c], x_recv.at[c], dev(far, m * 2 + h))
            item.start()
            x_copies.append(item)

    h_copies = {}

    def send_halo(c):
        if c == 0:
            h_copies[0] = []
            for t in range(4):
                await_bytes(vbuf.at[0, pl.ds(8, 2)], first_recv.at[t])
                for side in range(2):
                    for k in range(2):
                        at = 16 * side + 4 * k + t
                        item = copy(vbuf.at[0, 8 + 4 * k + t], vbuf.at[0, at], first_out.at[t, k, side],
                                    h_recv.at[0, side], dev(b, (down if side else up) * 2 + hi))
                        item.start()
                        h_copies[0].append(item)
            return
        await_bytes(vbuf.at[c, pl.ds(8, 8)], x_recv.at[c])
        own = vbuf.at[c, pl.ds(8, 8)]
        h_copies[c] = [
            copy(own, vbuf.at[c, pl.ds(0, 8)], h_send.at[c, 0], h_recv.at[c, 0], dev(b, up * 2 + hi)),
            copy(own, vbuf.at[c, pl.ds(16, 8)], h_send.at[c, 1], h_recv.at[c, 1], dev(b, down * 2 + hi)),
        ]
        for item in h_copies[c]:
            item.start()

    turn(0)
    zmat[...] = circulant()
    pl.semaphore_wait(barrier, len(peers))
    send_x(0)

    pot_load.wait()
    side = lax.rem(m + 2 * hi + 31, 32)
    pot_copies = [
        copy(pots.at[1 + hi], pots.at[1 + hi], pot_send.at[0], pot_recv, dev(b, m * 2 + 1 - hi)),
        copy(pots.at[1 + hi], pots.at[3 - 3 * hi], pot_send.at[1], pot_recv, dev(b, side * 2)),
        copy(pots.at[1 + hi], pots.at[3 - 3 * hi], pot_send.at[2], pot_recv, dev(b, side * 2 + 1)),
    ]
    for item in pot_copies:
        item.start()
    turn(1)
    send_x(1)
    turn(2)
    turn(3)
    send_halo(0)
    send_x(2)
    await_bytes(pots.at[pl.ds(0, 3)], pot_recv)
    for t in range(16):
        a = pots[t // 4, t % 4] * (1.0 / HALF) + (3.0 * TAPS[0] - CENTER / HALF)
        abuf[t] = jnp.broadcast_to(a[:, None, :], (8, 8, 128))
    send_halo(1)
    send_x(3)

    to_sib, to_far, relay = [], [], []

    def piece(plane, k):
        return gall.at[plane, k // 2, pl.ds(4 * (k % 2), 4)]

    def gather(lo, hi_):
        for k in range(lo, hi_):
            own = piece(b, k)
            to_far.append(copy(own, own, ga_send.at[1, k], ga_recv.at[1, k], dev(far, g)))
            to_sib.append(copy(own, own, ga_send.at[0, k], ga_recv.at[0, k], dev(sib, g)))
            to_far[k].start()
            to_sib[k].start()

    def pass_on(lo, hi_):
        for k in range(lo, hi_):
            to_far[k].wait_recv()
            theirs = piece(far, k)
            relay.append(copy(theirs, theirs, ga_send.at[2, k], ga_recv.at[2, k], dev(sib, g)))
            relay[k].start()

    a_copies = []
    row = far * 2 + hi
    for c in range(4):
        await_bytes(vbuf.at[c, pl.ds(0, 8)], h_recv.at[c, 0])
        await_bytes(vbuf.at[c, pl.ds(16, 8)], h_recv.at[c, 1])
        if c + 2 < 4:
            send_halo(c + 2)

        def first(i, _):
            t = i * GROUP
            ybuf[pl.ds(t, GROUP)] = stencil(lambda k: vbuf[c, pl.ds(t + 4 + k, GROUP)], abuf[pl.ds(t, GROUP)], zmat[...])
            return 0

        lax.fori_loop(0, 16 // GROUP, first, 0, unroll=2)
        for n in range(2):
            half = 1 - hi if n == 0 else hi
            t = half * 4
            step = stencil(lambda k: ybuf[pl.ds(t + 4 + k, 4)], abuf[pl.ds(t + 4, 4)], zmat[...])
            fbuf[c, pl.ds(t, 4)] = 2.0 * step - vbuf[c, pl.ds(t + 8, 4)]
            for i in range(n, 4):
                bb = lax.rem(b + i, 4)
                item = copy(fbuf.at[c, t + bb], gall.at[bb, c, row], a_send.at[c, 4 * n + i], a_recv.at[c], dev(bb, m * 2 + half))
                item.start()
                a_copies.append(item)
        pltpu.make_async_copy(fbuf.at[c, p], gall.at[b, c, row], a_recv.at[c]).start()
        if c >= 1:
            await_bytes(gall.at[b, c - 1], a_recv.at[c - 1])
        if c in (1, 2):
            gather(SPLIT[c - 1], SPLIT[c])
    await_bytes(gall.at[b, 3], a_recv.at[3])

    sends = []
    acc = None
    for pair in range(4):
        a = orbitals_of(gall, b, pair)
        term = nt(a, a)
        acc = term if acc is None else acc + term
    acc = acc * (1.0 / NCELLS)
    for half in range(2):
        mt[half] = acc[:, half * 128:half * 128 + 128].reshape(16, 2, 8, 128)
    item = copy(mt.at[1 - core], pair_in, pair_send, pair_recv, dev(sib, g))
    item.start()
    sends.append(item)

    sends[0].wait_recv()
    half_sum[...] = mt[core] + pair_in[...]
    for i in range(1, 16):
        q, target = layer(i)
        item = copy(half_sum.at[q], layer_in.at[i - 1], layer_send.at[i - 1], layer_recv, target)
        item.start()
        sends.append(item)
    gather(SPLIT[2], SPLIT[3])
    await_bytes(layer_in, layer_recv)
    total = half_sum[chip]
    for i in range(15):
        total = total + layer_in[i]
    zsum[z] = total
    for i in range(1, 8):
        q, target = zring(i)
        item = copy(zsum.at[z], zsum.at[z], z_send.at[i - 1], z_recv, target)
        item.start()
        sends.append(item)
    await_bytes(zsum.at[pl.ds(0, 7)], z_recv)
    total = zsum[0]
    for i in range(1, 8):
        total = total + zsum[i]
    mg[core, chip] = total
    for i in range(1, 16):
        q, target = layer(i)
        item = copy(mg.at[core, chip], mg.at[core, chip], spread_send.at[i - 1], spread_recv, target)
        item.start()
        sends.append(item)
    gather(SPLIT[3], 8)
    await_bytes(layer_in, spread_recv)
    item = copy(mg.at[core], mg.at[core], back_send, back_recv, dev(sib, g))
    item.start()
    sends.append(item)
    item.wait_recv()

    pass_on(0, SPLIT[3])
    w11 = inverse_factor(mg[0, 0:8].reshape(128, 128))
    pass_on(SPLIT[3], 6)
    l21 = nt(mg[0, 8:16].reshape(128, 128), w11)
    w22 = inverse_factor(mg[1, 8:16].reshape(128, 128) - nt(l21, l21))
    w[0:128, 0:128] = w11
    w[0:128, 128:256] = jnp.zeros((128, 128), jnp.float32)
    w[128:256, 0:128] = -nn(w22, nn(l21, w11))
    w[128:256, 128:256] = w22
    pass_on(6, 8)

    for k in range(8):
        to_sib[k].wait_recv()
        relay[k].wait_recv()
    for item in pot_copies + x_copies + a_copies + sends + to_sib + to_far + relay:
        item.wait_send()
    for c in range(4):
        for item in h_copies[c]:
            item.wait_send()


def inverse_factor(block):
    lane = lax.broadcasted_iota(jnp.int32, (8, 128), 1)
    sub = lax.broadcasted_iota(jnp.int32, (8, 128), 0)
    groups = [block[8 * i:8 * i + 8] for i in range(16)]
    for n in range(16):
        panel = groups[n]
        base = 8 * n
        d = [[None] * 8 for _ in range(8)]
        for j in range(8):
            column = jnp.broadcast_to(panel[:, base + j:base + j + 1], (8, 128))
            for i in range(j, 8):
                d[i][j] = jnp.broadcast_to(column[i:i + 1], (8, 128))
        inside = (lane >= base) & (lane < base + 8)
        masked = jnp.where(inside, jnp.where(lane == base + sub, 1.0, 0.0), panel)
        rows = [jnp.broadcast_to(masked[k:k + 1], (8, 128)) for k in range(8)]
        for j in range(8):
            r = lax.rsqrt(d[j][j])
            for i in range(j + 1, 8):
                d[i][j] = d[i][j] * r
            rows[j] = rows[j] * r
            for i in range(j + 1, 8):
                rows[i] = rows[i] - d[i][j] * rows[j]
                for k in range(j + 1, i + 1):
                    d[i][k] = d[i][k] - d[i][j] * d[k][j]
        out = rows[0]
        for k in range(1, 8):
            out = jnp.where(sub == k, rows[k], out)
        groups[n] = out
        for i in range(n + 1, 16):
            cur = jnp.where(inside, 0.0, groups[i])
            where = sub + 8 * i
            for j in range(8):
                cur = cur - jnp.take_along_axis(rows[j], where, axis=1) * rows[j]
            groups[i] = cur
    return jnp.concatenate([jnp.where(lane <= sub + 8 * i, groups[i], 0.0) for i in range(16)], axis=0)


def product_kernel(w, gall, out_hbm, res, out_sem):
    b = lax.axis_index("band")
    mine = w[pl.ds(pl.multiple_of(b * 64, 64), 64), :]
    outs = []
    for t in range(4):
        for pair in range(4):
            block = lax.dot_general(mine, orbitals_of(gall, t, pair), (((1,), (0,)), ((), ())), precision=lax.Precision.HIGH, preferred_element_type=jnp.float32)
            res[t, :, 2 * pair, :] = block[:, :128]
            res[t, :, 2 * pair + 1, :] = block[:, 128:]
        item = pltpu.make_async_copy(res.at[t], out_hbm.at[:, t], out_sem.at[t])
        item.start()
        outs.append(item)
    for item in outs:
        item.wait()


def body(orbitals, potential):
    f32 = jnp.float32
    dma = pltpu.SemaphoreType.DMA
    anywhere = functools.partial(pl.BlockSpec, memory_space=pl.ANY)
    vmem = functools.partial(pl.BlockSpec, memory_space=pltpu.VMEM)
    orbitals = pltpu.with_memory_space_constraint(orbitals, pltpu.HBM)
    potential = pltpu.with_memory_space_constraint(potential, pltpu.HBM)
    w, gall = pl.pallas_call(
        main_kernel,
        out_shape=(jax.ShapeDtypeStruct((256, 256), f32), jax.ShapeDtypeStruct((4, 4, 8, 8, 8, 128), f32)),
        in_specs=[anywhere(), anywhere()],
        out_specs=(vmem(), vmem()),
        scratch_shapes=[
            pltpu.VMEM((2, 4, 8, 4, 8, 128), f32),
            pltpu.VMEM((2, 4, 4, 8, 8, 128), f32),
            pltpu.VMEM((4, 24, 8, 8, 128), f32),
            pltpu.VMEM((16, 8, 8, 128), f32),
            pltpu.VMEM((16, 8, 8, 128), f32),
            pltpu.VMEM((4, 8, 8, 8, 128), f32),
            pltpu.VMEM((128, 128), f32),
            pltpu.VMEM((4, 4, 8, 128), f32),
            pltpu.VMEM((2, 16, 2, 8, 128), f32),
            pltpu.VMEM((16, 2, 8, 128), f32),
            pltpu.VMEM((16, 2, 8, 128), f32),
            pltpu.VMEM((15, 2, 8, 128), f32),
            pltpu.VMEM((8, 2, 8, 128), f32),
            pltpu.VMEM((2, 16, 2, 8, 128), f32),
            dma((2, 4)), dma,
            dma((3,)), dma,
            dma((2, 4)), dma((4,)),
            dma((2, 4)), dma((4,)), dma((4, 2, 2)),
            dma((4, 2)), dma((4, 2)),
            dma((4, 8)), dma((4,)),
            dma, dma,
            dma((15,)), dma,
            dma((7,)), dma,
            dma((15,)), dma,
            dma, dma,
            dma((3, 8)), dma((3, 8)),
        ],
        compiler_params=pltpu.CompilerParams(collective_id=0, has_side_effects=True, vmem_limit_bytes=40 * 2**20),
    )(orbitals, potential)
    return pl.pallas_call(
        product_kernel,
        out_shape=jax.ShapeDtypeStruct(orbitals.shape, f32),
        in_specs=[vmem(), vmem()],
        out_specs=anywhere(),
        scratch_shapes=[pltpu.VMEM((4, 64, 8, 128), f32), dma((4,))],
        compiler_params=pltpu.CompilerParams(vmem_limit_bytes=40 * 2**20),
    )(w, gall)


def solution(mesh):
    return jax.shard_map(
        body,
        mesh=mesh,
        in_specs=(P("band", "grid", None, None), P("grid", None, None)),
        out_specs=P("band", "grid", None, None),
        check_vma=False,
    )
```

```python
import functools

import jax
import jax.numpy as jnp
from jax import lax
from jax.experimental import pallas as pl
from jax.experimental.pallas import tpu as pltpu
from jax.sharding import PartitionSpec as P

MESH = pl.DeviceIdType.MESH
HIGH = lax.Precision.HIGHEST
COEFS = (-205.0 / 72.0, 8.0 / 5.0, -1.0 / 5.0, 8.0 / 315.0, -1.0 / 560.0)
CENTER = 8.0
HALF = 4.0
SCALE = -0.5 / HALF
TAPS = tuple(SCALE * c for c in COEFS)
NCELLS = 256 * 8 * 128
GROUP = 4

SPLIT = (0, 2, 2, 4)


def nt(a, b):
    return lax.dot_general(a, b, (((1,), (1,)), ((), ())), precision=HIGH, preferred_element_type=jnp.float32)


def nn(a, b):
    return lax.dot_general(a, b, (((1,), (0,)), ((), ())), precision=HIGH, preferred_element_type=jnp.float32)


def rotate_rows(c, k):
    return jnp.concatenate([c[:, k:], c[:, :k]], axis=1)


def circulant():
    i = lax.broadcasted_iota(jnp.int32, (128, 128), 0)
    j = lax.broadcasted_iota(jnp.int32, (128, 128), 1)
    apart = lax.rem(i - j + 128, 128)
    total = jnp.zeros((128, 128), jnp.float32)
    for k in range(1, 5):
        total = jnp.where((apart == k) | (apart == 128 - k), TAPS[k], total)
    return total


def stencil(read, coef, along_z):
    c = read(0)
    total = coef * c + nn(c.reshape(GROUP * 64, 128), along_z).reshape(GROUP, 8, 8, 128)
    for k in range(1, 5):
        s = read(-k) + read(k)
        s = s + (rotate_rows(c, k) + rotate_rows(c, 8 - k))
        total = total + TAPS[k] * s
    return total


def orbitals_of(gall, t, pair):
    return jnp.concatenate([
        jnp.concatenate([gall[t, c, slot, row] for slot in range(8) for c in range(4)], axis=0)
        for row in (2 * pair, 2 * pair + 1)], axis=1)


def main_kernel(orb_hbm, pot_hbm, w, gall, x_in, stage, vbuf, ybuf, abuf, fbuf, zmat, pots,
                mt, pair_in, half_sum, layer_in, zsum, mg,
                in_sem, pot_in, pot_send, pot_recv, x_send, x_recv, first_recv, h_send, h_recv, a_send, a_recv,
                pair_send, pair_recv, layer_send, layer_recv, z_send, z_recv,
                spread_send, spread_recv, back_send, back_recv, ga_send, ga_recv, far_recv):
    b = lax.axis_index("band")
    g = lax.axis_index("grid")
    hi = lax.rem(g, 2)
    m = g // 2
    y = lax.rem(m, 4)
    z = m // 4
    p = hi * 4 + b
    core = lax.rem(b, 2)
    chip = (y * 2 + hi) * 2 + b // 2
    up = lax.rem(m + 1, 32)
    down = lax.rem(m + 31, 32)

    def dev(bb, gg):
        return {"band": bb, "grid": gg}

    def copy(src, dst, ssem, rsem, target):
        return pltpu.make_async_remote_copy(src_ref=src, dst_ref=dst, send_sem=ssem, recv_sem=rsem,
                                            device_id=target, device_id_type=MESH)

    def await_bytes(ref, sem):
        pltpu.make_async_copy(ref, ref, sem).wait()

    def ring(i):
        q = lax.rem(p + i, 8)
        return q, dev(lax.rem(q, 4), m * 2 + q // 4)

    def layer(i):
        q = lax.rem(chip + i, 16)
        return q, dev(lax.rem(q, 2) * 2 + core, z * 8 + q // 2)

    def zring(i):
        zz = lax.rem(z + i, 8)
        return zz, dev(b, zz * 8 + y * 2 + hi)

    other = lax.rem(g + 63 + 2 * hi, 64)
    barrier = pltpu.get_barrier_semaphore()
    peers = [zring(i)[1] for i in (4, 3, 5, 2, 6, 1, 7)]
    peers += [layer(i)[1] for i in (10, 9, 11, 6, 14, 8, 2, 7, 13, 5, 3, 1, 4, 12, 15)]
    peers += [ring(i)[1] for i in range(1, 8)]
    peers += [dev(b, up * 2 + hi), dev(b, down * 2 + hi), dev(b, other)]
    for peer in peers:
        pl.semaphore_signal(barrier, inc=1, device_id=peer, device_id_type=MESH)

    pot_load = pltpu.make_async_copy(pot_hbm, pots.at[1 + hi], pot_in)
    pot_load.start()
    loads = []
    for c in range(4):
        for h in range(2):
            load = pltpu.make_async_copy(orb_hbm.at[pl.ds(h * 32 + c * 8, 8)], x_in.at[h, c], in_sem.at[h, c])
            load.start()
            loads.append(load)

    far = lax.rem(b + 2, 4)
    sib = b + 1 - 2 * core

    def turn(c):
        for h in range(2):
            loads[2 * c + h].wait()
            for plane in range(4):
                stage[h, c, plane] = jnp.swapaxes(x_in[h, c, :, plane], 0, 1)

    def send_x(c):
        for h in range(2):
            if c == 0:
                for t in range(4):
                    item = copy(stage.at[h, 0, t], vbuf.at[0, 8 + 4 * hi + t], x_send, first_recv.at[t], dev(far, m * 2 + h))
                    item.start()
                continue
            item = copy(stage.at[h, c], vbuf.at[c, pl.ds(8 + 4 * hi, 4)], x_send, x_recv.at[c], dev(far, m * 2 + h))
            item.start()

    def send_halo(c):
        if c == 0:
            for t in range(4):
                await_bytes(vbuf.at[0, pl.ds(8, 2)], first_recv.at[t])
                for side in range(2):
                    for k in range(2):
                        at = 16 * side + 4 * k + t
                        item = copy(vbuf.at[0, 8 + 4 * k + t], vbuf.at[0, at], h_send.at[0],
                                    h_recv.at[0, side], dev(b, (down if side else up) * 2 + hi))
                        item.start()
            return
        await_bytes(vbuf.at[c, pl.ds(8, 8)], x_recv.at[c])
        own = vbuf.at[c, pl.ds(8, 8)]
        copy(own, vbuf.at[c, pl.ds(0, 8)], h_send.at[c], h_recv.at[c, 0], dev(b, up * 2 + hi)).start()
        copy(own, vbuf.at[c, pl.ds(16, 8)], h_send.at[c], h_recv.at[c, 1], dev(b, down * 2 + hi)).start()

    turn(0)
    zmat[...] = circulant()
    pl.semaphore_wait(barrier, len(peers))
    send_x(0)

    pot_load.wait()
    side = lax.rem(m + 2 * hi + 31, 32)
    pot_copies = [
        copy(pots.at[1 + hi], pots.at[1 + hi], pot_send, pot_recv, dev(b, m * 2 + 1 - hi)),
        copy(pots.at[1 + hi], pots.at[3 - 3 * hi], pot_send, pot_recv, dev(b, side * 2)),
        copy(pots.at[1 + hi], pots.at[3 - 3 * hi], pot_send, pot_recv, dev(b, side * 2 + 1)),
    ]
    for item in pot_copies:
        item.start()
    turn(1)
    send_x(1)
    turn(2)
    turn(3)
    send_halo(0)
    send_x(2)
    await_bytes(pots.at[pl.ds(0, 3)], pot_recv)
    for t in range(16):
        a = pots[t // 4, t % 4] * (1.0 / HALF) + (3.0 * TAPS[0] - CENTER / HALF)
        abuf[t] = jnp.broadcast_to(a[:, None, :], (8, 8, 128))
    send_halo(1)
    send_x(3)

    to_sib, to_far, relay = [], [], []

    def piece(plane, k):
        return gall.at[plane, k // 2, pl.ds(4 * (k % 2), 4)]

    def gather(lo, hi_):
        for k in range(lo, hi_):
            own = piece(b, k)
            to_far.append(copy(own, own, ga_send.at[1], far_recv.at[k], dev(far, g)))
            to_sib.append(copy(own, own, ga_send.at[0], ga_recv.at[0], dev(sib, g)))
            to_far[k].start()
            to_sib[k].start()

    def pass_on(lo, hi_):
        for k in range(lo, hi_):
            to_far[k].wait_recv()
            theirs = piece(far, k)
            relay.append(copy(theirs, theirs, ga_send.at[2], ga_recv.at[1], dev(sib, g)))
            relay[k].start()

    row = far * 2 + hi
    for c in range(4):
        await_bytes(vbuf.at[c, pl.ds(0, 8)], h_recv.at[c, 0])
        await_bytes(vbuf.at[c, pl.ds(16, 8)], h_recv.at[c, 1])
        if c + 2 < 4:
            send_halo(c + 2)

        def first(i, _):
            t = i * GROUP
            ybuf[pl.ds(t, GROUP)] = stencil(lambda k: vbuf[c, pl.ds(t + 4 + k, GROUP)], abuf[pl.ds(t, GROUP)], zmat[...])
            return 0

        lax.fori_loop(0, 16 // GROUP, first, 0, unroll=2)
        for n in range(2):
            half = 1 - hi if n == 0 else hi
            t = half * 4
            step = stencil(lambda k: ybuf[pl.ds(t + 4 + k, 4)], abuf[pl.ds(t + 4, 4)], zmat[...])
            fbuf[c, pl.ds(t, 4)] = 2.0 * step - vbuf[c, pl.ds(t + 8, 4)]
            for i in range(n, 4):
                bb = lax.rem(b + i, 4)
                item = copy(fbuf.at[c, t + bb], gall.at[bb, c, row], a_send.at[c], a_recv.at[c], dev(bb, m * 2 + half))
                item.start()
        pltpu.make_async_copy(fbuf.at[c, p], gall.at[b, c, row], a_recv.at[c]).start()
        if c >= 1:
            await_bytes(gall.at[b, c - 1], a_recv.at[c - 1])
        if c in (1, 2):
            gather(SPLIT[c - 1], SPLIT[c])
    await_bytes(gall.at[b, 3], a_recv.at[3])

    acc = None
    for pair in range(4):
        a = orbitals_of(gall, b, pair)
        term = nt(a, a)
        acc = term if acc is None else acc + term
    acc = acc * (1.0 / NCELLS)
    for half in range(2):
        mt[half] = acc[:, half * 128:half * 128 + 128].reshape(16, 2, 8, 128)
    item = copy(mt.at[1 - core], pair_in, pair_send, pair_recv, dev(sib, g))
    item.start()

    item.wait_recv()
    half_sum[...] = mt[core] + pair_in[...]
    for i in range(1, 16):
        q, target = layer(i)
        item = copy(half_sum.at[q], layer_in.at[i - 1], layer_send, layer_recv, target)
        item.start()
    gather(SPLIT[2], SPLIT[3])
    await_bytes(layer_in, layer_recv)
    total = half_sum[chip]
    for i in range(15):
        total = total + layer_in[i]
    zsum[z] = total
    for i in range(1, 8):
        q, target = zring(i)
        item = copy(zsum.at[z], zsum.at[z], z_send, z_recv, target)
        item.start()
    await_bytes(zsum.at[pl.ds(0, 7)], z_recv)
    total = zsum[0]
    for i in range(1, 8):
        total = total + zsum[i]
    mg[core, chip] = total
    for i in range(1, 16):
        q, target = layer(i)
        item = copy(mg.at[core, chip], mg.at[core, chip], spread_send, spread_recv, target)
        item.start()
    gather(SPLIT[3], 8)
    await_bytes(pots.at[pl.ds(0, 3)], pot_send)
    await_bytes(stage, x_send)
    for c in range(4):
        await_bytes(vbuf.at[c, pl.ds(0, 16)], h_send.at[c])
        await_bytes(fbuf.at[c, pl.ds(0, 7)], a_send.at[c])
    await_bytes(mt.at[0], pair_send)
    await_bytes(layer_in, layer_send)
    await_bytes(zsum.at[pl.ds(0, 7)], z_send)
    await_bytes(layer_in, spread_recv)
    item = copy(mg.at[core], mg.at[core], back_send, back_recv, dev(sib, g))
    item.start()
    item.wait_recv()

    pass_on(0, SPLIT[3])
    w11 = inverse_factor(mg[0, 0:8].reshape(128, 128))
    pass_on(SPLIT[3], 6)
    l21 = nt(mg[0, 8:16].reshape(128, 128), w11)
    w22 = inverse_factor(mg[1, 8:16].reshape(128, 128) - nt(l21, l21))
    w[0:128, 0:128] = w11
    w[0:128, 128:256] = jnp.zeros((128, 128), jnp.float32)
    w[128:256, 0:128] = -nn(w22, nn(l21, w11))
    w[128:256, 128:256] = w22
    pass_on(6, 8)

    await_bytes(layer_in, spread_send)
    await_bytes(mt.at[0], back_send)
    await_bytes(gall.at[sib], ga_recv.at[0])
    await_bytes(gall.at[lax.rem(sib + 2, 4)], ga_recv.at[1])
    for k in range(3):
        await_bytes(gall.at[b], ga_send.at[k])


def inverse_factor(block):
    lane = lax.broadcasted_iota(jnp.int32, (8, 128), 1)
    sub = lax.broadcasted_iota(jnp.int32, (8, 128), 0)
    groups = [block[8 * i:8 * i + 8] for i in range(16)]
    for n in range(16):
        panel = groups[n]
        base = 8 * n
        d = [[None] * 8 for _ in range(8)]
        for j in range(8):
            column = jnp.broadcast_to(panel[:, base + j:base + j + 1], (8, 128))
            for i in range(j, 8):
                d[i][j] = jnp.broadcast_to(column[i:i + 1], (8, 128))
        inside = (lane >= base) & (lane < base + 8)
        masked = jnp.where(inside, jnp.where(lane == base + sub, 1.0, 0.0), panel)
        rows = [jnp.broadcast_to(masked[k:k + 1], (8, 128)) for k in range(8)]
        for j in range(8):
            r = lax.rsqrt(d[j][j])
            for i in range(j + 1, 8):
                d[i][j] = d[i][j] * r
            rows[j] = rows[j] * r
            for i in range(j + 1, 8):
                rows[i] = rows[i] - d[i][j] * rows[j]
                for k in range(j + 1, i + 1):
                    d[i][k] = d[i][k] - d[i][j] * d[k][j]
        out = rows[0]
        for k in range(1, 8):
            out = jnp.where(sub == k, rows[k], out)
        groups[n] = out
        for i in range(n + 1, 16):
            cur = jnp.where(inside, 0.0, groups[i])
            where = sub + 8 * i
            for j in range(8):
                cur = cur - jnp.take_along_axis(rows[j], where, axis=1) * rows[j]
            groups[i] = cur
    return jnp.concatenate([jnp.where(lane <= sub + 8 * i, groups[i], 0.0) for i in range(16)], axis=0)


def split(a):
    top = a.astype(jnp.bfloat16)
    return top, (a - top.astype(jnp.float32)).astype(jnp.bfloat16)


def product_kernel(w, gall, out_hbm, res, out_sem):
    b = lax.axis_index("band")
    mine = jnp.concatenate(split(w[pl.ds(pl.multiple_of(b * 64, 64), 64), :]), axis=0)
    outs = []
    for t in range(4):
        for pair in range(4):
            top, low = split(orbitals_of(gall, t, pair))
            dims = (((1,), (0,)), ((), ()))
            both = (lax.dot_general(mine, top, dims, preferred_element_type=jnp.float32)
                    + lax.dot_general(mine, low, dims, preferred_element_type=jnp.float32))
            block = both[:64] + both[64:]
            res[t, :, 2 * pair, :] = block[:, :128]
            res[t, :, 2 * pair + 1, :] = block[:, 128:]
        item = pltpu.make_async_copy(res.at[t], out_hbm.at[:, t], out_sem.at[t])
        item.start()
        outs.append(item)
    for item in outs:
        item.wait()


def body(orbitals, potential):
    f32 = jnp.float32
    dma = pltpu.SemaphoreType.DMA
    anywhere = functools.partial(pl.BlockSpec, memory_space=pl.ANY)
    vmem = functools.partial(pl.BlockSpec, memory_space=pltpu.VMEM)
    orbitals = pltpu.with_memory_space_constraint(orbitals, pltpu.HBM)
    potential = pltpu.with_memory_space_constraint(potential, pltpu.HBM)
    w, gall = pl.pallas_call(
        main_kernel,
        out_shape=(jax.ShapeDtypeStruct((256, 256), f32), jax.ShapeDtypeStruct((4, 4, 8, 8, 8, 128), f32)),
        in_specs=[anywhere(), anywhere()],
        out_specs=(vmem(), vmem()),
        scratch_shapes=[
            pltpu.VMEM((2, 4, 8, 4, 8, 128), f32),
            pltpu.VMEM((2, 4, 4, 8, 8, 128), f32),
            pltpu.VMEM((4, 24, 8, 8, 128), f32),
            pltpu.VMEM((16, 8, 8, 128), f32),
            pltpu.VMEM((16, 8, 8, 128), f32),
            pltpu.VMEM((4, 8, 8, 8, 128), f32),
            pltpu.VMEM((128, 128), f32),
            pltpu.VMEM((4, 4, 8, 128), f32),
            pltpu.VMEM((2, 16, 2, 8, 128), f32),
            pltpu.VMEM((16, 2, 8, 128), f32),
            pltpu.VMEM((16, 2, 8, 128), f32),
            pltpu.VMEM((15, 2, 8, 128), f32),
            pltpu.VMEM((8, 2, 8, 128), f32),
            pltpu.VMEM((2, 16, 2, 8, 128), f32),
            dma((2, 4)), dma,
            dma, dma,
            dma, dma((4,)),
            dma((4,)),
            dma((4,)), dma((4, 2)),
            dma((4,)), dma((4,)),
            dma, dma,
            dma, dma,
            dma, dma,
            dma, dma,
            dma, dma,
            dma((3,)), dma((2,)), dma((8,)),
        ],
        compiler_params=pltpu.CompilerParams(collective_id=0, has_side_effects=True, vmem_limit_bytes=40 * 2**20),
    )(orbitals, potential)
    return pl.pallas_call(
        product_kernel,
        out_shape=jax.ShapeDtypeStruct(orbitals.shape, f32),
        in_specs=[vmem(), vmem()],
        out_specs=anywhere(),
        scratch_shapes=[pltpu.VMEM((4, 64, 8, 128), f32), dma((4,))],
        compiler_params=pltpu.CompilerParams(vmem_limit_bytes=40 * 2**20),
    )(w, gall)


def solution(mesh):
    return jax.shard_map(
        body,
        mesh=mesh,
        in_specs=(P("band", "grid", None, None), P("grid", None, None)),
        out_specs=P("band", "grid", None, None),
        check_vma=False,
    )
```

```python
import functools

import jax
import jax.numpy as jnp
from jax import lax
from jax.experimental import pallas as pl
from jax.experimental.pallas import tpu as pltpu
from jax.sharding import PartitionSpec as P

MESH = pl.DeviceIdType.MESH
HIGH = lax.Precision.HIGHEST
COEFS = (-205.0 / 72.0, 8.0 / 5.0, -1.0 / 5.0, 8.0 / 315.0, -1.0 / 560.0)
CENTER = 8.0
HALF = 4.0
SCALE = -0.5 / HALF
TAPS = tuple(SCALE * c for c in COEFS)
NCELLS = 256 * 8 * 128
GROUP = 4

SPLIT = (0, 2, 2, 4)


def nt(a, b):
    return lax.dot_general(a, b, (((1,), (1,)), ((), ())), precision=HIGH, preferred_element_type=jnp.float32)


def nn(a, b):
    return lax.dot_general(a, b, (((1,), (0,)), ((), ())), precision=HIGH, preferred_element_type=jnp.float32)


def rotate_rows(c, k):
    return jnp.concatenate([c[:, k:], c[:, :k]], axis=1)


def circulant():
    i = lax.broadcasted_iota(jnp.int32, (128, 128), 0)
    j = lax.broadcasted_iota(jnp.int32, (128, 128), 1)
    apart = (i - j) & 127
    total = jnp.zeros((128, 128), jnp.float32)
    for k in range(1, 5):
        total = jnp.where((apart == k) | (apart == 128 - k), TAPS[k], total)
    return total


def stencil(read, coef, along_z):
    c = read(0)
    total = coef * c + nn(c.reshape(GROUP * 64, 128), along_z).reshape(GROUP, 8, 8, 128)
    for k in range(1, 5):
        s = read(-k) + read(k)
        s = s + (rotate_rows(c, k) + rotate_rows(c, 8 - k))
        total = total + TAPS[k] * s
    return total


def orbitals_of(gall, t, pair):
    return jnp.concatenate([
        jnp.concatenate([gall[t, c, slot, row] for slot in range(8) for c in range(4)], axis=0)
        for row in (2 * pair, 2 * pair + 1)], axis=1)


def main_kernel(orb_hbm, pot_hbm, w, gall, x_in, stage, vbuf, ybuf, abuf, fbuf, zmat, pots,
                mt, pair_in, half_sum, layer_in, zsum, mg, columns,
                in_sem, pot_in, pot_send, pot_recv, x_send, x_recv, first_recv, h_send, h_recv, a_send, a_recv,
                pair_send, pair_recv, layer_send, layer_recv, z_send, z_recv,
                spread_send, spread_recv, back_send, back_recv, ga_send, ga_recv, far_recv):
    b = lax.axis_index("band")
    g = lax.axis_index("grid")
    hi = lax.rem(g, 2)
    m = g // 2
    y = lax.rem(m, 4)
    z = m // 4
    p = hi * 4 + b
    core = lax.rem(b, 2)
    chip = (y * 2 + hi) * 2 + b // 2
    up = lax.rem(m + 1, 32)
    down = lax.rem(m + 31, 32)

    def dev(bb, gg):
        return {"band": bb, "grid": gg}

    def copy(src, dst, ssem, rsem, target):
        return pltpu.make_async_remote_copy(src_ref=src, dst_ref=dst, send_sem=ssem, recv_sem=rsem,
                                            device_id=target, device_id_type=MESH)

    def await_bytes(ref, sem):
        pltpu.make_async_copy(ref, ref, sem).wait()

    def ring(i):
        q = lax.rem(p + i, 8)
        return q, dev(lax.rem(q, 4), m * 2 + q // 4)

    def layer(i):
        q = lax.rem(chip + i, 16)
        return q, dev(lax.rem(q, 2) * 2 + core, z * 8 + q // 2)

    def zring(i):
        zz = lax.rem(z + i, 8)
        return zz, dev(b, zz * 8 + y * 2 + hi)

    loads = []

    def load(lo, hi_):
        for c in range(lo, hi_):
            for h in range(2):
                item = pltpu.make_async_copy(orb_hbm.at[pl.ds(h * 32 + c * 8, 8)], x_in.at[h, c], in_sem.at[h, c])
                item.start()
                loads.append(item)

    load(0, 1)
    other = lax.rem(g + 63 + 2 * hi, 64)
    barrier = pltpu.get_barrier_semaphore()
    peers = [zring(i)[1] for i in (4, 3, 5, 2, 6, 1, 7)]
    peers += [layer(i)[1] for i in (10, 9, 11, 6, 14, 8, 2, 7, 13, 5, 3, 1, 4, 12, 15)]
    peers += [ring(i)[1] for i in range(1, 8)]
    peers += [dev(b, up * 2 + hi), dev(b, down * 2 + hi), dev(b, other)]
    for peer in peers:
        pl.semaphore_signal(barrier, inc=1, device_id=peer, device_id_type=MESH)

    load(1, 4)
    pot_load = pltpu.make_async_copy(pot_hbm, pots.at[1 + hi], pot_in)
    pot_load.start()

    far = lax.rem(b + 2, 4)
    sib = b + 1 - 2 * core

    def turn(c):
        for h in range(2):
            loads[2 * c + h].wait()
            for plane in range(4):
                stage[h, c, plane] = jnp.swapaxes(x_in[h, c, :, plane], 0, 1)

    def send_x(c):
        for h in range(2):
            if c == 0:
                for t in range(4):
                    item = copy(stage.at[h, 0, t], vbuf.at[0, 8 + 4 * hi + t], x_send, first_recv.at[t], dev(far, m * 2 + h))
                    item.start()
                continue
            item = copy(stage.at[h, c], vbuf.at[c, pl.ds(8 + 4 * hi, 4)], x_send, x_recv.at[c], dev(far, m * 2 + h))
            item.start()

    def send_halo(c):
        if c == 0:
            for t in range(4):
                await_bytes(vbuf.at[0, pl.ds(8, 2)], first_recv.at[t])
                for side in range(2):
                    for k in range(2):
                        at = 16 * side + 4 * k + t
                        item = copy(vbuf.at[0, 8 + 4 * k + t], vbuf.at[0, at], h_send.at[0],
                                    h_recv.at[0, side], dev(b, (down if side else up) * 2 + hi))
                        item.start()
            return
        await_bytes(vbuf.at[c, pl.ds(8, 8)], x_recv.at[c])
        own = vbuf.at[c, pl.ds(8, 8)]
        copy(own, vbuf.at[c, pl.ds(0, 8)], h_send.at[c], h_recv.at[c, 0], dev(b, up * 2 + hi)).start()
        copy(own, vbuf.at[c, pl.ds(16, 8)], h_send.at[c], h_recv.at[c, 1], dev(b, down * 2 + hi)).start()

    turn(0)
    pl.semaphore_wait(barrier, len(peers))
    send_x(0)

    pot_load.wait()
    side = lax.rem(m + 2 * hi + 31, 32)
    pot_copies = [
        copy(pots.at[1 + hi], pots.at[1 + hi], pot_send, pot_recv, dev(b, m * 2 + 1 - hi)),
        copy(pots.at[1 + hi], pots.at[3 - 3 * hi], pot_send, pot_recv, dev(b, side * 2)),
        copy(pots.at[1 + hi], pots.at[3 - 3 * hi], pot_send, pot_recv, dev(b, side * 2 + 1)),
    ]
    for item in pot_copies:
        item.start()
    turn(1)
    send_x(1)
    turn(2)
    turn(3)
    send_halo(0)
    send_x(2)
    zmat[...] = circulant()
    await_bytes(pots.at[pl.ds(0, 3)], pot_recv)
    for t in range(16):
        a = pots[t // 4, t % 4] * (1.0 / HALF) + (3.0 * TAPS[0] - CENTER / HALF)
        abuf[t] = jnp.broadcast_to(a[:, None, :], (8, 8, 128))
    send_halo(1)
    send_x(3)

    to_sib, to_far, relay = [], [], []

    def piece(plane, k):
        return gall.at[plane, k // 2, pl.ds(4 * (k % 2), 4)]

    def gather(lo, hi_):
        for k in range(lo, hi_):
            own = piece(b, k)
            to_far.append(copy(own, own, ga_send.at[1], far_recv.at[k], dev(far, g)))
            to_sib.append(copy(own, own, ga_send.at[0], ga_recv.at[0], dev(sib, g)))
            to_far[k].start()
            to_sib[k].start()

    def pass_on(lo, hi_):
        for k in range(lo, hi_):
            to_far[k].wait_recv()
            theirs = piece(far, k)
            relay.append(copy(theirs, theirs, ga_send.at[2], ga_recv.at[1], dev(sib, g)))
            relay[k].start()

    row = far * 2 + hi
    for c in range(4):
        await_bytes(vbuf.at[c, pl.ds(0, 8)], h_recv.at[c, 0])
        await_bytes(vbuf.at[c, pl.ds(16, 8)], h_recv.at[c, 1])
        if c + 2 < 4:
            send_halo(c + 2)

        def first(i, _):
            t = i * GROUP
            ybuf[pl.ds(t, GROUP)] = stencil(lambda k: vbuf[c, pl.ds(t + 4 + k, GROUP)], abuf[pl.ds(t, GROUP)], zmat[...])
            return 0

        lax.fori_loop(0, 16 // GROUP, first, 0, unroll=2)
        for n in range(2):
            half = 1 - hi if n == 0 else hi
            t = half * 4
            step = stencil(lambda k: ybuf[pl.ds(t + 4 + k, 4)], abuf[pl.ds(t + 4, 4)], zmat[...])
            fbuf[c, pl.ds(t, 4)] = 2.0 * step - vbuf[c, pl.ds(t + 8, 4)]
            for i in range(n, 4):
                bb = lax.rem(b + i, 4)
                item = copy(fbuf.at[c, t + bb], gall.at[bb, c, row], a_send.at[c], a_recv.at[c], dev(bb, m * 2 + half))
                item.start()
        pltpu.make_async_copy(fbuf.at[c, p], gall.at[b, c, row], a_recv.at[c]).start()
        if c >= 1:
            await_bytes(gall.at[b, c - 1], a_recv.at[c - 1])
        if c in (1, 2):
            gather(SPLIT[c - 1], SPLIT[c])
    await_bytes(gall.at[b, 3], a_recv.at[3])

    acc = None
    for pair in range(4):
        a = orbitals_of(gall, b, pair)
        term = nt(a, a)
        acc = term if acc is None else acc + term
    acc = acc * (1.0 / NCELLS)
    for half in range(2):
        mt[half] = acc[:, half * 128:half * 128 + 128].reshape(16, 2, 8, 128)
    item = copy(mt.at[1 - core], pair_in, pair_send, pair_recv, dev(sib, g))
    item.start()

    item.wait_recv()
    half_sum[...] = mt[core] + pair_in[...]
    for i in range(1, 16):
        q, target = layer(i)
        item = copy(half_sum.at[q], layer_in.at[i - 1], layer_send, layer_recv, target)
        item.start()
    gather(SPLIT[2], SPLIT[3])
    await_bytes(layer_in, layer_recv)
    total = half_sum[chip]
    for i in range(15):
        total = total + layer_in[i]
    zsum[z] = total
    for i in range(1, 8):
        q, target = zring(i)
        item = copy(zsum.at[z], zsum.at[z], z_send, z_recv, target)
        item.start()
    await_bytes(zsum.at[pl.ds(0, 7)], z_recv)
    total = zsum[0]
    for i in range(1, 8):
        total = total + zsum[i]
    mg[core, chip] = total
    for i in range(1, 16):
        q, target = layer(i)
        item = copy(mg.at[core, chip], mg.at[core, chip], spread_send, spread_recv, target)
        item.start()
    gather(SPLIT[3], 8)
    await_bytes(pots.at[pl.ds(0, 3)], pot_send)
    await_bytes(stage, x_send)
    for c in range(4):
        await_bytes(vbuf.at[c, pl.ds(0, 16)], h_send.at[c])
        await_bytes(fbuf.at[c, pl.ds(0, 7)], a_send.at[c])
    await_bytes(mt.at[0], pair_send)
    await_bytes(layer_in, layer_send)
    await_bytes(zsum.at[pl.ds(0, 7)], z_send)
    await_bytes(layer_in, spread_recv)
    item = copy(mg.at[core], mg.at[core], back_send, back_recv, dev(sib, g))
    item.start()
    item.wait_recv()

    pass_on(0, SPLIT[3])
    w11 = inverse_factor(mg[0, 0:8].reshape(128, 128), columns)
    pass_on(SPLIT[3], 6)
    l21 = nt(mg[0, 8:16].reshape(128, 128), w11)
    w22 = inverse_factor(mg[1, 8:16].reshape(128, 128) - nt(l21, l21), columns)
    w[0:128, 0:128] = w11
    w[0:128, 128:256] = jnp.zeros((128, 128), jnp.float32)
    w[128:256, 0:128] = -nn(w22, nn(l21, w11))
    w[128:256, 128:256] = w22
    pass_on(6, 8)

    await_bytes(layer_in, spread_send)
    await_bytes(mt.at[0], back_send)
    await_bytes(gall.at[sib], ga_recv.at[0])
    await_bytes(gall.at[lax.rem(sib + 2, 4)], ga_recv.at[1])
    for k in range(3):
        await_bytes(gall.at[b], ga_send.at[k])


def inverse_factor(block, columns):
    lane = lax.broadcasted_iota(jnp.int32, (8, 128), 1)
    sub = lax.broadcasted_iota(jnp.int32, (8, 128), 0)
    groups = [block[8 * i:8 * i + 8] for i in range(16)]
    for n in range(16):
        panel = groups[n]
        base = 8 * n
        d = [[None] * 8 for _ in range(8)]
        for j in range(8):
            column = jnp.broadcast_to(panel[:, base + j:base + j + 1], (8, 128))
            columns[n % 2, j] = column
            for i in range(j, 8):
                d[i][j] = columns[n % 2, j, pl.ds(i, 8, stride=0), :]
        inside = (lane >= base) & (lane < base + 8)
        masked = jnp.where(inside, jnp.where(lane == base + sub, 1.0, 0.0), panel)
        rows = [jnp.broadcast_to(masked[k:k + 1], (8, 128)) for k in range(8)]
        for j in range(8):
            r = lax.rsqrt(d[j][j])
            for i in range(j + 1, 8):
                d[i][j] = d[i][j] * r
            rows[j] = rows[j] * r
            for i in range(j + 1, 8):
                rows[i] = rows[i] - d[i][j] * rows[j]
                for k in range(j + 1, i + 1):
                    d[i][k] = d[i][k] - d[i][j] * d[k][j]
        out = rows[0]
        for k in range(1, 8):
            out = jnp.where(sub == k, rows[k], out)
        groups[n] = out
        for i in range(n + 1, 16):
            cur = jnp.where(inside, 0.0, groups[i])
            where = sub + 8 * i
            for j in range(8):
                cur = cur - jnp.take_along_axis(rows[j], where, axis=1) * rows[j]
            groups[i] = cur
    return jnp.concatenate([jnp.where(lane <= sub + 8 * i, groups[i], 0.0) for i in range(16)], axis=0)


def split(a):
    top = a.astype(jnp.bfloat16)
    return top, (a - top.astype(jnp.float32)).astype(jnp.bfloat16)


def product_kernel(w, gall, out_hbm, res, out_sem):
    b = lax.axis_index("band")
    mine = jnp.concatenate(split(w[pl.ds(pl.multiple_of(b * 64, 64), 64), :]), axis=0)
    outs = []
    for t in range(4):
        for pair in range(4):
            top, low = split(orbitals_of(gall, t, pair))
            dims = (((1,), (0,)), ((), ()))
            both = (lax.dot_general(mine, top, dims, preferred_element_type=jnp.float32)
                    + lax.dot_general(mine, low, dims, preferred_element_type=jnp.float32))
            block = both[:64] + both[64:]
            res[t, :, 2 * pair, :] = block[:, :128]
            res[t, :, 2 * pair + 1, :] = block[:, 128:]
        item = pltpu.make_async_copy(res.at[t], out_hbm.at[:, t], out_sem.at[t])
        item.start()
        outs.append(item)
    for item in outs:
        item.wait()


def body(orbitals, potential):
    f32 = jnp.float32
    dma = pltpu.SemaphoreType.DMA
    anywhere = functools.partial(pl.BlockSpec, memory_space=pl.ANY)
    vmem = functools.partial(pl.BlockSpec, memory_space=pltpu.VMEM)
    orbitals = pltpu.with_memory_space_constraint(orbitals, pltpu.HBM)
    potential = pltpu.with_memory_space_constraint(potential, pltpu.HBM)
    w, gall = pl.pallas_call(
        main_kernel,
        out_shape=(jax.ShapeDtypeStruct((256, 256), f32), jax.ShapeDtypeStruct((4, 4, 8, 8, 8, 128), f32)),
        in_specs=[anywhere(), anywhere()],
        out_specs=(vmem(), vmem()),
        scratch_shapes=[
            pltpu.VMEM((2, 4, 8, 4, 8, 128), f32),
            pltpu.VMEM((2, 4, 4, 8, 8, 128), f32),
            pltpu.VMEM((4, 24, 8, 8, 128), f32),
            pltpu.VMEM((16, 8, 8, 128), f32),
            pltpu.VMEM((16, 8, 8, 128), f32),
            pltpu.VMEM((4, 8, 8, 8, 128), f32),
            pltpu.VMEM((128, 128), f32),
            pltpu.VMEM((4, 4, 8, 128), f32),
            pltpu.VMEM((2, 16, 2, 8, 128), f32),
            pltpu.VMEM((16, 2, 8, 128), f32),
            pltpu.VMEM((16, 2, 8, 128), f32),
            pltpu.VMEM((15, 2, 8, 128), f32),
            pltpu.VMEM((8, 2, 8, 128), f32),
            pltpu.VMEM((2, 16, 2, 8, 128), f32),
            pltpu.VMEM((2, 8, 8, 128), f32),
            dma((2, 4)), dma,
            dma, dma,
            dma, dma((4,)),
            dma((4,)),
            dma((4,)), dma((4, 2)),
            dma((4,)), dma((4,)),
            dma, dma,
            dma, dma,
            dma, dma,
            dma, dma,
            dma, dma,
            dma((3,)), dma((2,)), dma((8,)),
        ],
        compiler_params=pltpu.CompilerParams(collective_id=0, has_side_effects=True, vmem_limit_bytes=40 * 2**20),
    )(orbitals, potential)
    return pl.pallas_call(
        product_kernel,
        out_shape=jax.ShapeDtypeStruct(orbitals.shape, f32),
        in_specs=[vmem(), vmem()],
        out_specs=anywhere(),
        scratch_shapes=[pltpu.VMEM((4, 64, 8, 128), f32), dma((4,))],
        compiler_params=pltpu.CompilerParams(vmem_limit_bytes=40 * 2**20),
    )(w, gall)


def solution(mesh):
    return jax.shard_map(
        body,
        mesh=mesh,
        in_specs=(P("band", "grid", None, None), P("grid", None, None)),
        out_specs=P("band", "grid", None, None),
        check_vma=False,
    )
```

```python
import functools

import jax
import jax.numpy as jnp
from jax import lax
from jax.experimental import pallas as pl
from jax.experimental.pallas import tpu as pltpu
from jax.sharding import PartitionSpec as P

MESH = pl.DeviceIdType.MESH
HIGH = lax.Precision.HIGHEST
COEFS = (-205.0 / 72.0, 8.0 / 5.0, -1.0 / 5.0, 8.0 / 315.0, -1.0 / 560.0)
CENTER = 8.0
HALF = 4.0
SCALE = -0.5 / HALF
TAPS = tuple(SCALE * c for c in COEFS)
NCELLS = 256 * 8 * 128
GROUP = 4

SPLIT = (0, 2, 2, 4)


def nt(a, b):
    return lax.dot_general(a, b, (((1,), (1,)), ((), ())), precision=HIGH, preferred_element_type=jnp.float32)


def nn(a, b):
    return lax.dot_general(a, b, (((1,), (0,)), ((), ())), precision=HIGH, preferred_element_type=jnp.float32)


def rotate_rows(c, k):
    return jnp.concatenate([c[:, k:], c[:, :k]], axis=1)


def circulant():
    i = lax.broadcasted_iota(jnp.int32, (128, 128), 0)
    j = lax.broadcasted_iota(jnp.int32, (128, 128), 1)
    apart = (i - j) & 127
    total = jnp.zeros((128, 128), jnp.float32)
    for k in range(1, 5):
        total = jnp.where((apart == k) | (apart == 128 - k), TAPS[k], total)
    return total


def stencil(read, coef, along_z):
    c = read(0)
    total = coef * c + nn(c.reshape(GROUP * 64, 128), along_z).reshape(GROUP, 8, 8, 128)
    for k in range(1, 5):
        s = read(-k) + read(k)
        s = s + (rotate_rows(c, k) + rotate_rows(c, 8 - k))
        total = total + TAPS[k] * s
    return total


def orbitals_of(gall, t, pair):
    return jnp.concatenate([
        jnp.concatenate([gall[t, c, slot, row] for slot in range(8) for c in range(4)], axis=0)
        for row in (2 * pair, 2 * pair + 1)], axis=1)


def main_kernel(orb_hbm, pot_hbm, w, gall, x_in, stage, vbuf, ybuf, abuf, fbuf, zmat, pots,
                mt, pair_in, half_sum, layer_in, zsum, mg, columns,
                in_sem, pot_in, pot_send, pot_recv, x_send, x_recv, first_recv, h_send, h_recv, a_send, a_recv,
                pair_send, pair_recv, layer_send, layer_recv, z_send, z_recv,
                spread_send, spread_recv, back_send, back_recv, ga_send, ga_recv, far_recv):
    b = lax.axis_index("band")
    g = lax.axis_index("grid")
    hi = lax.rem(g, 2)
    m = g // 2
    y = lax.rem(m, 4)
    z = m // 4
    p = hi * 4 + b
    core = lax.rem(b, 2)
    chip = (y * 2 + hi) * 2 + b // 2
    up = lax.rem(m + 1, 32)
    down = lax.rem(m + 31, 32)

    def dev(bb, gg):
        return {"band": bb, "grid": gg}

    def copy(src, dst, ssem, rsem, target):
        return pltpu.make_async_remote_copy(src_ref=src, dst_ref=dst, send_sem=ssem, recv_sem=rsem,
                                            device_id=target, device_id_type=MESH)

    def await_bytes(ref, sem):
        pltpu.make_async_copy(ref, ref, sem).wait()

    def ring(i):
        q = lax.rem(p + i, 8)
        return q, dev(lax.rem(q, 4), m * 2 + q // 4)

    def layer(i):
        q = lax.rem(chip + i, 16)
        return q, dev(lax.rem(q, 2) * 2 + core, z * 8 + q // 2)

    def zring(i):
        zz = lax.rem(z + i, 8)
        return zz, dev(b, zz * 8 + y * 2 + hi)

    loads = []

    def load(lo, hi_):
        for c in range(lo, hi_):
            for h in range(2):
                item = pltpu.make_async_copy(orb_hbm.at[pl.ds(h * 32 + c * 8, 8)], x_in.at[h, c], in_sem.at[h, c])
                item.start()
                loads.append(item)

    load(0, 1)
    other = lax.rem(g + 63 + 2 * hi, 64)
    barrier = pltpu.get_barrier_semaphore()
    peers = [zring(i)[1] for i in (4, 3, 5, 2, 6, 1, 7)]
    peers += [layer(i)[1] for i in (10, 9, 11, 6, 14, 8, 2, 7, 13, 5, 3, 1, 4, 12, 15)]
    peers += [ring(i)[1] for i in range(1, 8)]
    peers += [dev(b, up * 2 + hi), dev(b, down * 2 + hi), dev(b, other)]
    for peer in peers:
        pl.semaphore_signal(barrier, inc=1, device_id=peer, device_id_type=MESH)

    load(1, 4)
    pot_load = pltpu.make_async_copy(pot_hbm, pots.at[1 + hi], pot_in)
    pot_load.start()

    far = lax.rem(b + 2, 4)
    sib = b + 1 - 2 * core

    def turn(c):
        for h in range(2):
            loads[2 * c + h].wait()
            for plane in range(4):
                stage[h, c, plane] = jnp.swapaxes(x_in[h, c, :, plane], 0, 1)

    def send_x(c):
        for h in range(2):
            if c == 0:
                for t in range(4):
                    item = copy(stage.at[h, 0, t], vbuf.at[0, 8 + 4 * hi + t], x_send, first_recv.at[t], dev(far, m * 2 + h))
                    item.start()
                continue
            item = copy(stage.at[h, c], vbuf.at[c, pl.ds(8 + 4 * hi, 4)], x_send, x_recv.at[c], dev(far, m * 2 + h))
            item.start()

    def send_halo(c):
        if c == 0:
            for t in range(4):
                await_bytes(vbuf.at[0, pl.ds(8, 2)], first_recv.at[t])
                for side in range(2):
                    for k in range(2):
                        at = 16 * side + 4 * k + t
                        item = copy(vbuf.at[0, 8 + 4 * k + t], vbuf.at[0, at], h_send.at[0],
                                    h_recv.at[0, side], dev(b, (down if side else up) * 2 + hi))
                        item.start()
            return
        await_bytes(vbuf.at[c, pl.ds(8, 8)], x_recv.at[c])
        own = vbuf.at[c, pl.ds(8, 8)]
        copy(own, vbuf.at[c, pl.ds(0, 8)], h_send.at[c], h_recv.at[c, 0], dev(b, up * 2 + hi)).start()
        copy(own, vbuf.at[c, pl.ds(16, 8)], h_send.at[c], h_recv.at[c, 1], dev(b, down * 2 + hi)).start()

    turn(0)
    pl.semaphore_wait(barrier, len(peers))
    send_x(0)

    pot_load.wait()
    side = lax.rem(m + 2 * hi + 31, 32)
    pot_copies = [
        copy(pots.at[1 + hi], pots.at[1 + hi], pot_send, pot_recv, dev(b, m * 2 + 1 - hi)),
        copy(pots.at[1 + hi], pots.at[3 - 3 * hi], pot_send, pot_recv, dev(b, side * 2)),
        copy(pots.at[1 + hi], pots.at[3 - 3 * hi], pot_send, pot_recv, dev(b, side * 2 + 1)),
    ]
    for item in pot_copies:
        item.start()
    turn(1)
    send_x(1)
    turn(2)
    turn(3)
    send_halo(0)
    send_x(2)
    zmat[...] = circulant()
    await_bytes(pots.at[pl.ds(0, 3)], pot_recv)
    for t in range(16):
        a = pots[t // 4, t % 4] * (1.0 / HALF) + (3.0 * TAPS[0] - CENTER / HALF)
        abuf[t] = jnp.broadcast_to(a[:, None, :], (8, 8, 128))
    send_halo(1)
    send_x(3)

    to_sib, to_far, relay = [], [], []

    def piece(plane, k):
        return gall.at[plane, k // 2, pl.ds(4 * (k % 2), 4)]

    def gather(lo, hi_):
        for k in range(lo, hi_):
            own = piece(b, k)
            to_far.append(copy(own, own, ga_send.at[1], far_recv.at[k], dev(far, g)))
            to_sib.append(copy(own, own, ga_send.at[0], ga_recv.at[0], dev(sib, g)))
            to_far[k].start()
            to_sib[k].start()

    def pass_on(lo, hi_):
        for k in range(lo, hi_):
            to_far[k].wait_recv()
            theirs = piece(far, k)
            relay.append(copy(theirs, theirs, ga_send.at[2], ga_recv.at[1], dev(sib, g)))
            relay[k].start()

    row = far * 2 + hi
    for c in range(4):
        await_bytes(vbuf.at[c, pl.ds(0, 8)], h_recv.at[c, 0])
        await_bytes(vbuf.at[c, pl.ds(16, 8)], h_recv.at[c, 1])
        if c + 2 < 4:
            send_halo(c + 2)

        def first(i, _):
            t = i * GROUP
            ybuf[pl.ds(t, GROUP)] = stencil(lambda k: vbuf[c, pl.ds(t + 4 + k, GROUP)], abuf[pl.ds(t, GROUP)], zmat[...])
            return 0

        lax.fori_loop(0, 16 // GROUP, first, 0, unroll=2)
        for n in range(2):
            half = 1 - hi if n == 0 else hi
            t = half * 4
            step = stencil(lambda k: ybuf[pl.ds(t + 4 + k, 4)], abuf[pl.ds(t + 4, 4)], zmat[...])
            fbuf[c, pl.ds(t, 4)] = 2.0 * step - vbuf[c, pl.ds(t + 8, 4)]
            for i in range(n, 4):
                bb = lax.rem(b + i, 4)
                item = copy(fbuf.at[c, t + bb], gall.at[bb, c, row], a_send.at[c], a_recv.at[c], dev(bb, m * 2 + half))
                item.start()
        pltpu.make_async_copy(fbuf.at[c, p], gall.at[b, c, row], a_recv.at[c]).start()
        if c >= 1:
            await_bytes(gall.at[b, c - 1], a_recv.at[c - 1])
        if c in (1, 2):
            gather(SPLIT[c - 1], SPLIT[c])
    await_bytes(gall.at[b, 3], a_recv.at[3])

    acc = None
    for pair in range(4):
        a = orbitals_of(gall, b, pair)
        term = nt(a, a)
        acc = term if acc is None else acc + term
    acc = acc * (1.0 / NCELLS)
    for half in range(2):
        mt[half] = acc[:, half * 128:half * 128 + 128].reshape(16, 2, 8, 128)
    item = copy(mt.at[1 - core], pair_in, pair_send, pair_recv, dev(sib, g))
    item.start()

    item.wait_recv()
    half_sum[...] = mt[core] + pair_in[...]
    for i in range(1, 16):
        q, target = layer(i)
        item = copy(half_sum.at[q], layer_in.at[i - 1], layer_send, layer_recv, target)
        item.start()
    gather(SPLIT[2], SPLIT[3])
    await_bytes(layer_in, layer_recv)
    total = half_sum[chip]
    for i in range(15):
        total = total + layer_in[i]
    zsum[z] = total
    for i in range(1, 8):
        q, target = zring(i)
        item = copy(zsum.at[z], zsum.at[z], z_send, z_recv, target)
        item.start()
    await_bytes(zsum.at[pl.ds(0, 7)], z_recv)
    total = zsum[0]
    for i in range(1, 8):
        total = total + zsum[i]
    mg[core, chip] = total
    for i in range(1, 16):
        q, target = layer(i)
        item = copy(mg.at[core, chip], mg.at[core, chip], spread_send, spread_recv, target)
        item.start()
    gather(SPLIT[3], 8)
    await_bytes(pots.at[pl.ds(0, 3)], pot_send)
    await_bytes(stage, x_send)
    for c in range(4):
        await_bytes(vbuf.at[c, pl.ds(0, 16)], h_send.at[c])
        await_bytes(fbuf.at[c, pl.ds(0, 7)], a_send.at[c])
    await_bytes(mt.at[0], pair_send)
    await_bytes(layer_in, layer_send)
    await_bytes(zsum.at[pl.ds(0, 7)], z_send)
    await_bytes(layer_in, spread_recv)
    item = copy(mg.at[core], mg.at[core], back_send, back_recv, dev(sib, g))
    item.start()
    item.wait_recv()

    pass_on(0, SPLIT[3])
    w11 = inverse_factor(mg[0, 0:8].reshape(128, 128), columns)
    pass_on(SPLIT[3], 6)
    l21 = nt(mg[0, 8:16].reshape(128, 128), w11)
    w22 = inverse_factor(mg[1, 8:16].reshape(128, 128) - nt(l21, l21), columns)
    w[0:128, 0:128] = w11
    w[0:128, 128:256] = jnp.zeros((128, 128), jnp.float32)
    w[128:256, 0:128] = -nn(w22, nn(l21, w11))
    w[128:256, 128:256] = w22
    pass_on(6, 8)

    await_bytes(layer_in, spread_send)
    await_bytes(mt.at[0], back_send)
    await_bytes(gall.at[sib], ga_recv.at[0])
    await_bytes(gall.at[lax.rem(sib + 2, 4)], ga_recv.at[1])
    for k in range(3):
        await_bytes(gall.at[b], ga_send.at[k])


def inverse_factor(block, columns):
    lane = lax.broadcasted_iota(jnp.int32, (8, 128), 1)
    sub = lax.broadcasted_iota(jnp.int32, (8, 128), 0)
    groups = [block[8 * i:8 * i + 8] for i in range(16)]
    for n in range(16):
        panel = groups[n]
        base = 8 * n
        d = [[None] * 8 for _ in range(8)]
        for j in range(8):
            column = jnp.broadcast_to(panel[:, base + j:base + j + 1], (8, 128))
            columns[n % 2, j, 0:8] = column
            for i in range(j, 8):
                d[i][j] = columns[n % 2, j, pl.ds(i, 8, stride=0), :]
        inside = (lane >= base) & (lane < base + 8)
        masked = jnp.where(inside, jnp.where(lane == base + sub, 1.0, 0.0), panel)
        rows = [jnp.broadcast_to(masked[k:k + 1], (8, 128)) for k in range(8)]
        for j in range(8):
            r = lax.rsqrt(d[j][j])
            for i in range(j + 1, 8):
                d[i][j] = d[i][j] * r
            rows[j] = rows[j] * r
            for i in range(j + 1, 8):
                rows[i] = rows[i] - d[i][j] * rows[j]
                for k in range(j + 1, i + 1):
                    d[i][k] = d[i][k] - d[i][j] * d[k][j]
        out = rows[0]
        for k in range(1, 8):
            out = jnp.where(sub == k, rows[k], out)
        groups[n] = out
        for i in range(n + 1, 16):
            cur = jnp.where(inside, 0.0, groups[i])
            where = sub + 8 * i
            for j in range(8):
                cur = cur - jnp.take_along_axis(rows[j], where, axis=1) * rows[j]
            groups[i] = cur
    return jnp.concatenate([jnp.where(lane <= sub + 8 * i, groups[i], 0.0) for i in range(16)], axis=0)


def split(a):
    top = a.astype(jnp.bfloat16)
    return top, (a - top.astype(jnp.float32)).astype(jnp.bfloat16)


def product_kernel(w, gall, out_hbm, res, out_sem):
    b = lax.axis_index("band")
    mine = jnp.concatenate(split(w[pl.ds(pl.multiple_of(b * 64, 64), 64), :]), axis=0)
    outs = []
    for t in range(4):
        for pair in range(4):
            top, low = split(orbitals_of(gall, t, pair))
            dims = (((1,), (0,)), ((), ()))
            both = (lax.dot_general(mine, top, dims, preferred_element_type=jnp.float32)
                    + lax.dot_general(mine, low, dims, preferred_element_type=jnp.float32))
            block = both[:64] + both[64:]
            res[t, :, 2 * pair, :] = block[:, :128]
            res[t, :, 2 * pair + 1, :] = block[:, 128:]
        item = pltpu.make_async_copy(res.at[t], out_hbm.at[:, t], out_sem.at[t])
        item.start()
        outs.append(item)
    for item in outs:
        item.wait()


def body(orbitals, potential):
    f32 = jnp.float32
    dma = pltpu.SemaphoreType.DMA
    anywhere = functools.partial(pl.BlockSpec, memory_space=pl.ANY)
    vmem = functools.partial(pl.BlockSpec, memory_space=pltpu.VMEM)
    orbitals = pltpu.with_memory_space_constraint(orbitals, pltpu.HBM)
    potential = pltpu.with_memory_space_constraint(potential, pltpu.HBM)
    w, gall = pl.pallas_call(
        main_kernel,
        out_shape=(jax.ShapeDtypeStruct((256, 256), f32), jax.ShapeDtypeStruct((4, 4, 8, 8, 8, 128), f32)),
        in_specs=[anywhere(), anywhere()],
        out_specs=(vmem(), vmem()),
        scratch_shapes=[
            pltpu.VMEM((2, 4, 8, 4, 8, 128), f32),
            pltpu.VMEM((2, 4, 4, 8, 8, 128), f32),
            pltpu.VMEM((4, 24, 8, 8, 128), f32),
            pltpu.VMEM((16, 8, 8, 128), f32),
            pltpu.VMEM((16, 8, 8, 128), f32),
            pltpu.VMEM((4, 8, 8, 8, 128), f32),
            pltpu.VMEM((128, 128), f32),
            pltpu.VMEM((4, 4, 8, 128), f32),
            pltpu.VMEM((2, 16, 2, 8, 128), f32),
            pltpu.VMEM((16, 2, 8, 128), f32),
            pltpu.VMEM((16, 2, 8, 128), f32),
            pltpu.VMEM((15, 2, 8, 128), f32),
            pltpu.VMEM((8, 2, 8, 128), f32),
            pltpu.VMEM((2, 16, 2, 8, 128), f32),
            pltpu.VMEM((2, 8, 16, 128), f32),
            dma((2, 4)), dma,
            dma, dma,
            dma, dma((4,)),
            dma((4,)),
            dma((4,)), dma((4, 2)),
            dma((4,)), dma((4,)),
            dma, dma,
            dma, dma,
            dma, dma,
            dma, dma,
            dma, dma,
            dma((3,)), dma((2,)), dma((8,)),
        ],
        compiler_params=pltpu.CompilerParams(collective_id=0, has_side_effects=True, vmem_limit_bytes=40 * 2**20),
    )(orbitals, potential)
    return pl.pallas_call(
        product_kernel,
        out_shape=jax.ShapeDtypeStruct(orbitals.shape, f32),
        in_specs=[vmem(), vmem()],
        out_specs=anywhere(),
        scratch_shapes=[pltpu.VMEM((4, 64, 8, 128), f32), dma((4,))],
        compiler_params=pltpu.CompilerParams(vmem_limit_bytes=40 * 2**20),
    )(w, gall)


def solution(mesh):
    return jax.shard_map(
        body,
        mesh=mesh,
        in_specs=(P("band", "grid", None, None), P("grid", None, None)),
        out_specs=P("band", "grid", None, None),
        check_vma=False,
    )
```

```python
import functools

import jax
import jax.numpy as jnp
from jax import lax
from jax.experimental import pallas as pl
from jax.experimental.pallas import tpu as pltpu
from jax.sharding import PartitionSpec as P

MESH = pl.DeviceIdType.MESH
HIGH = lax.Precision.HIGHEST
COEFS = (-205.0 / 72.0, 8.0 / 5.0, -1.0 / 5.0, 8.0 / 315.0, -1.0 / 560.0)
CENTER = 8.0
HALF = 4.0
SCALE = -0.5 / HALF
TAPS = tuple(SCALE * c for c in COEFS)
NCELLS = 256 * 8 * 128
GROUP = 4

SPLIT = (0, 2, 2, 4)


def nt(a, b):
    return lax.dot_general(a, b, (((1,), (1,)), ((), ())), precision=HIGH, preferred_element_type=jnp.float32)


def nn(a, b):
    return lax.dot_general(a, b, (((1,), (0,)), ((), ())), precision=HIGH, preferred_element_type=jnp.float32)


def rotate_rows(c, k):
    return jnp.concatenate([c[:, k:], c[:, :k]], axis=1)


def circulant():
    i = lax.broadcasted_iota(jnp.int32, (128, 128), 0)
    j = lax.broadcasted_iota(jnp.int32, (128, 128), 1)
    apart = (i - j) & 127
    total = jnp.zeros((128, 128), jnp.float32)
    for k in range(1, 5):
        total = jnp.where((apart == k) | (apart == 128 - k), TAPS[k], total)
    return total


def stencil(read, coef, along_z):
    c = read(0)
    total = coef * c + nn(c.reshape(GROUP * 64, 128), along_z).reshape(GROUP, 8, 8, 128)
    for k in range(1, 5):
        s = read(-k) + read(k)
        s = s + (rotate_rows(c, k) + rotate_rows(c, 8 - k))
        total = total + TAPS[k] * s
    return total


def orbitals_of(gall, t, pair):
    return jnp.concatenate([
        jnp.concatenate([gall[t, c, slot, row] for slot in range(8) for c in range(4)], axis=0)
        for row in (2 * pair, 2 * pair + 1)], axis=1)


def main_kernel(orb_hbm, pot_hbm, w, gall, x_in, stage, vbuf, ybuf, abuf, fbuf, zmat, pots,
                mt, pair_in, half_sum, layer_in, zsum, mg, columns,
                in_sem, pot_in, pot_send, pot_recv, x_send, x_recv, first_recv, h_send, h_recv, a_send, a_recv,
                pair_send, pair_recv, layer_send, layer_recv, z_send, z_recv,
                spread_send, spread_recv, back_send, back_recv, ga_send, ga_recv, far_recv):
    b = lax.axis_index("band")
    g = lax.axis_index("grid")
    hi = lax.rem(g, 2)
    m = g // 2
    y = lax.rem(m, 4)
    z = m // 4
    p = hi * 4 + b
    core = lax.rem(b, 2)
    chip = (y * 2 + hi) * 2 + b // 2
    up = lax.rem(m + 1, 32)
    down = lax.rem(m + 31, 32)

    def dev(bb, gg):
        return {"band": bb, "grid": gg}

    def copy(src, dst, ssem, rsem, target):
        return pltpu.make_async_remote_copy(src_ref=src, dst_ref=dst, send_sem=ssem, recv_sem=rsem,
                                            device_id=target, device_id_type=MESH)

    def await_bytes(ref, sem):
        pltpu.make_async_copy(ref, ref, sem).wait()

    def ring(i):
        q = lax.rem(p + i, 8)
        return q, dev(lax.rem(q, 4), m * 2 + q // 4)

    def layer(i):
        q = lax.rem(chip + i, 16)
        return q, dev(lax.rem(q, 2) * 2 + core, z * 8 + q // 2)

    def zring(i):
        zz = lax.rem(z + i, 8)
        return zz, dev(b, zz * 8 + y * 2 + hi)

    loads = []

    def load(lo, hi_):
        for c in range(lo, hi_):
            for h in range(2):
                item = pltpu.make_async_copy(orb_hbm.at[pl.ds(h * 32 + c * 8, 8)], x_in.at[h, c], in_sem.at[h, c])
                item.start()
                loads.append(item)

    load(0, 1)
    other = lax.rem(g + 63 + 2 * hi, 64)
    barrier = pltpu.get_barrier_semaphore()
    peers = [zring(i)[1] for i in (4, 3, 5, 2, 6, 1, 7)]
    peers += [layer(i)[1] for i in (10, 9, 11, 6, 14, 8, 2, 7, 13, 5, 3, 1, 4, 12, 15)]
    peers += [ring(i)[1] for i in range(1, 8)]
    peers += [dev(b, up * 2 + hi), dev(b, down * 2 + hi), dev(b, other)]
    for peer in peers:
        pl.semaphore_signal(barrier, inc=1, device_id=peer, device_id_type=MESH)

    load(1, 4)
    pot_load = pltpu.make_async_copy(pot_hbm, pots.at[1 + hi], pot_in)
    pot_load.start()

    far = lax.rem(b + 2, 4)
    sib = b + 1 - 2 * core

    def turn(c):
        for h in range(2):
            loads[2 * c + h].wait()
            for plane in range(4):
                stage[h, c, plane] = jnp.swapaxes(x_in[h, c, :, plane], 0, 1)

    def send_x(c):
        for h in range(2):
            if c == 0:
                for t in range(4):
                    item = copy(stage.at[h, 0, t], vbuf.at[0, 8 + 4 * hi + t], x_send, first_recv.at[t], dev(far, m * 2 + h))
                    item.start()
                continue
            item = copy(stage.at[h, c], vbuf.at[c, pl.ds(8 + 4 * hi, 4)], x_send, x_recv.at[c], dev(far, m * 2 + h))
            item.start()

    def send_halo(c):
        if c == 0:
            for t in range(4):
                await_bytes(vbuf.at[0, pl.ds(8, 2)], first_recv.at[t])
                for side in range(2):
                    for k in range(2):
                        at = 16 * side + 4 * k + t
                        item = copy(vbuf.at[0, 8 + 4 * k + t], vbuf.at[0, at], h_send.at[0],
                                    h_recv.at[0, side], dev(b, (down if side else up) * 2 + hi))
                        item.start()
            return
        await_bytes(vbuf.at[c, pl.ds(8, 8)], x_recv.at[c])
        own = vbuf.at[c, pl.ds(8, 8)]
        copy(own, vbuf.at[c, pl.ds(0, 8)], h_send.at[c], h_recv.at[c, 0], dev(b, up * 2 + hi)).start()
        copy(own, vbuf.at[c, pl.ds(16, 8)], h_send.at[c], h_recv.at[c, 1], dev(b, down * 2 + hi)).start()

    turn(0)
    pl.semaphore_wait(barrier, len(peers))
    send_x(0)

    pot_load.wait()
    side = lax.rem(m + 2 * hi + 31, 32)
    pot_copies = [
        copy(pots.at[1 + hi], pots.at[1 + hi], pot_send, pot_recv, dev(b, m * 2 + 1 - hi)),
        copy(pots.at[1 + hi], pots.at[3 - 3 * hi], pot_send, pot_recv, dev(b, side * 2)),
        copy(pots.at[1 + hi], pots.at[3 - 3 * hi], pot_send, pot_recv, dev(b, side * 2 + 1)),
    ]
    for item in pot_copies:
        item.start()
    turn(1)
    send_x(1)
    turn(2)
    turn(3)
    send_halo(0)
    send_x(2)
    zmat[...] = circulant()
    await_bytes(pots.at[pl.ds(0, 3)], pot_recv)
    for t in range(16):
        a = pots[t // 4, t % 4] * (1.0 / HALF) + (3.0 * TAPS[0] - CENTER / HALF)
        abuf[t] = jnp.broadcast_to(a[:, None, :], (8, 8, 128))
    send_halo(1)
    send_x(3)

    to_sib, to_far, relay = [], [], []

    def piece(plane, k):
        return gall.at[plane, k // 2, pl.ds(4 * (k % 2), 4)]

    def gather(lo, hi_):
        for k in range(lo, hi_):
            own = piece(b, k)
            to_far.append(copy(own, own, ga_send.at[1], far_recv.at[k], dev(far, g)))
            to_sib.append(copy(own, own, ga_send.at[0], ga_recv.at[0], dev(sib, g)))
            to_far[k].start()
            to_sib[k].start()

    def pass_on(lo, hi_):
        for k in range(lo, hi_):
            to_far[k].wait_recv()
            theirs = piece(far, k)
            relay.append(copy(theirs, theirs, ga_send.at[2], ga_recv.at[1], dev(sib, g)))
            relay[k].start()

    row = far * 2 + hi
    for c in range(4):
        await_bytes(vbuf.at[c, pl.ds(0, 8)], h_recv.at[c, 0])
        await_bytes(vbuf.at[c, pl.ds(16, 8)], h_recv.at[c, 1])
        if c + 2 < 4:
            send_halo(c + 2)

        def first(i, _):
            t = i * GROUP
            ybuf[pl.ds(t, GROUP)] = stencil(lambda k: vbuf[c, pl.ds(t + 4 + k, GROUP)], abuf[pl.ds(t, GROUP)], zmat[...])
            return 0

        lax.fori_loop(0, 16 // GROUP, first, 0, unroll=2)
        for n in range(2):
            half = 1 - hi if n == 0 else hi
            t = half * 4
            step = stencil(lambda k: ybuf[pl.ds(t + 4 + k, 4)], abuf[pl.ds(t + 4, 4)], zmat[...])
            fbuf[c, pl.ds(t, 4)] = 2.0 * step - vbuf[c, pl.ds(t + 8, 4)]
            for i in range(n, 4):
                bb = lax.rem(b + i, 4)
                item = copy(fbuf.at[c, t + bb], gall.at[bb, c, row], a_send.at[c], a_recv.at[c], dev(bb, m * 2 + half))
                item.start()
        pltpu.make_async_copy(fbuf.at[c, p], gall.at[b, c, row], a_recv.at[c]).start()
        if c >= 1:
            await_bytes(gall.at[b, c - 1], a_recv.at[c - 1])
        if c in (1, 2):
            gather(SPLIT[c - 1], SPLIT[c])
    await_bytes(gall.at[b, 3], a_recv.at[3])

    acc = None
    for pair in range(4):
        a = orbitals_of(gall, b, pair)
        term = nt(a, a)
        acc = term if acc is None else acc + term
    acc = acc * (1.0 / NCELLS)
    for half in range(2):
        mt[half] = acc[:, half * 128:half * 128 + 128].reshape(16, 2, 8, 128)
    item = copy(mt.at[1 - core], pair_in, pair_send, pair_recv, dev(sib, g))
    item.start()

    item.wait_recv()
    half_sum[...] = mt[core] + pair_in[...]
    for i in range(1, 16):
        q, target = layer(i)
        item = copy(half_sum.at[q], layer_in.at[i - 1], layer_send, layer_recv, target)
        item.start()
    gather(SPLIT[2], SPLIT[3])
    await_bytes(layer_in, layer_recv)
    total = half_sum[chip]
    for i in range(15):
        total = total + layer_in[i]
    zsum[z] = total
    for i in range(1, 8):
        q, target = zring(i)
        item = copy(zsum.at[z], zsum.at[z], z_send, z_recv, target)
        item.start()
    await_bytes(zsum.at[pl.ds(0, 7)], z_recv)
    total = zsum[0]
    for i in range(1, 8):
        total = total + zsum[i]
    mg[core, chip] = total
    for i in range(1, 16):
        q, target = layer(i)
        item = copy(mg.at[core, chip], mg.at[core, chip], spread_send, spread_recv, target)
        item.start()
    gather(SPLIT[3], 8)
    await_bytes(pots.at[pl.ds(0, 3)], pot_send)
    await_bytes(stage, x_send)
    for c in range(4):
        await_bytes(vbuf.at[c, pl.ds(0, 16)], h_send.at[c])
        await_bytes(fbuf.at[c, pl.ds(0, 7)], a_send.at[c])
    await_bytes(mt.at[0], pair_send)
    await_bytes(layer_in, layer_send)
    await_bytes(zsum.at[pl.ds(0, 7)], z_send)
    await_bytes(layer_in, spread_recv)
    item = copy(mg.at[core], mg.at[core], back_send, back_recv, dev(sib, g))
    item.start()
    item.wait_recv()

    pass_on(0, SPLIT[3])
    w11 = inverse_factor(mg[0, 0:8].reshape(128, 128), columns)
    pass_on(SPLIT[3], 6)
    l21 = nt(mg[0, 8:16].reshape(128, 128), w11)
    cross = nn(l21, w11)
    w22 = inverse_factor(mg[1, 8:16].reshape(128, 128) - nt(l21, l21), columns)
    w[0:128, 0:128] = w11
    w[0:128, 128:256] = jnp.zeros((128, 128), jnp.float32)
    w[128:256, 0:128] = -nn(w22, cross)
    w[128:256, 128:256] = w22
    pass_on(6, 8)

    await_bytes(layer_in, spread_send)
    await_bytes(mt.at[0], back_send)
    await_bytes(gall.at[sib], ga_recv.at[0])
    await_bytes(gall.at[lax.rem(sib + 2, 4)], ga_recv.at[1])
    for k in range(3):
        await_bytes(gall.at[b], ga_send.at[k])


def inverse_factor(block, columns):
    lane = lax.broadcasted_iota(jnp.int32, (8, 128), 1)
    sub = lax.broadcasted_iota(jnp.int32, (8, 128), 0)
    groups = [block[8 * i:8 * i + 8] for i in range(16)]
    for n in range(16):
        panel = groups[n]
        base = 8 * n
        d = [[None] * 8 for _ in range(8)]
        for j in range(8):
            column = jnp.broadcast_to(panel[:, base + j:base + j + 1], (8, 128))
            columns[n % 2, j, 0:8] = column
            for i in range(j, 8):
                d[i][j] = columns[n % 2, j, pl.ds(i, 8, stride=0), :]
        inside = (lane >= base) & (lane < base + 8)
        masked = jnp.where(inside, jnp.where(lane == base + sub, 1.0, 0.0), panel)
        rows = [jnp.broadcast_to(masked[k:k + 1], (8, 128)) for k in range(8)]
        for j in range(8):
            r = lax.rsqrt(d[j][j])
            for i in range(j + 1, 8):
                d[i][j] = d[i][j] * r
            rows[j] = rows[j] * r
            for i in range(j + 1, 8):
                rows[i] = rows[i] - d[i][j] * rows[j]
                for k in range(j + 1, i + 1):
                    d[i][k] = d[i][k] - d[i][j] * d[k][j]
        out = rows[0]
        for k in range(1, 8):
            out = jnp.where(sub == k, rows[k], out)
        groups[n] = out
        for i in range(n + 1, 16):
            cur = jnp.where(inside, 0.0, groups[i])
            where = sub + 8 * i
            for j in range(8):
                cur = cur - jnp.take_along_axis(rows[j], where, axis=1) * rows[j]
            groups[i] = cur
    return jnp.concatenate([jnp.where(lane <= sub + 8 * i, groups[i], 0.0) for i in range(16)], axis=0)


def split(a):
    top = a.astype(jnp.bfloat16)
    return top, (a - top.astype(jnp.float32)).astype(jnp.bfloat16)


def product_kernel(w, gall, out_hbm, res, out_sem):
    b = lax.axis_index("band")
    mine = jnp.concatenate(split(w[pl.ds(pl.multiple_of(b * 64, 64), 64), :]), axis=0)
    outs = []
    for t in range(4):
        for pair in range(4):
            top, low = split(orbitals_of(gall, t, pair))
            dims = (((1,), (0,)), ((), ()))
            both = (lax.dot_general(mine, top, dims, preferred_element_type=jnp.float32)
                    + lax.dot_general(mine, low, dims, preferred_element_type=jnp.float32))
            block = both[:64] + both[64:]
            res[t, :, 2 * pair, :] = block[:, :128]
            res[t, :, 2 * pair + 1, :] = block[:, 128:]
        item = pltpu.make_async_copy(res.at[t], out_hbm.at[:, t], out_sem.at[t])
        item.start()
        outs.append(item)
    for item in outs:
        item.wait()


def body(orbitals, potential):
    f32 = jnp.float32
    dma = pltpu.SemaphoreType.DMA
    anywhere = functools.partial(pl.BlockSpec, memory_space=pl.ANY)
    vmem = functools.partial(pl.BlockSpec, memory_space=pltpu.VMEM)
    orbitals = pltpu.with_memory_space_constraint(orbitals, pltpu.HBM)
    potential = pltpu.with_memory_space_constraint(potential, pltpu.HBM)
    w, gall = pl.pallas_call(
        main_kernel,
        out_shape=(jax.ShapeDtypeStruct((256, 256), f32), jax.ShapeDtypeStruct((4, 4, 8, 8, 8, 128), f32)),
        in_specs=[anywhere(), anywhere()],
        out_specs=(vmem(), vmem()),
        scratch_shapes=[
            pltpu.VMEM((2, 4, 8, 4, 8, 128), f32),
            pltpu.VMEM((2, 4, 4, 8, 8, 128), f32),
            pltpu.VMEM((4, 24, 8, 8, 128), f32),
            pltpu.VMEM((16, 8, 8, 128), f32),
            pltpu.VMEM((16, 8, 8, 128), f32),
            pltpu.VMEM((4, 8, 8, 8, 128), f32),
            pltpu.VMEM((128, 128), f32),
            pltpu.VMEM((4, 4, 8, 128), f32),
            pltpu.VMEM((2, 16, 2, 8, 128), f32),
            pltpu.VMEM((16, 2, 8, 128), f32),
            pltpu.VMEM((16, 2, 8, 128), f32),
            pltpu.VMEM((15, 2, 8, 128), f32),
            pltpu.VMEM((8, 2, 8, 128), f32),
            pltpu.VMEM((2, 16, 2, 8, 128), f32),
            pltpu.VMEM((2, 8, 16, 128), f32),
            dma((2, 4)), dma,
            dma, dma,
            dma, dma((4,)),
            dma((4,)),
            dma((4,)), dma((4, 2)),
            dma((4,)), dma((4,)),
            dma, dma,
            dma, dma,
            dma, dma,
            dma, dma,
            dma, dma,
            dma((3,)), dma((2,)), dma((8,)),
        ],
        compiler_params=pltpu.CompilerParams(collective_id=0, has_side_effects=True, vmem_limit_bytes=40 * 2**20),
    )(orbitals, potential)
    return pl.pallas_call(
        product_kernel,
        out_shape=jax.ShapeDtypeStruct(orbitals.shape, f32),
        in_specs=[vmem(), vmem()],
        out_specs=anywhere(),
        scratch_shapes=[pltpu.VMEM((4, 64, 8, 128), f32), dma((4,))],
        compiler_params=pltpu.CompilerParams(vmem_limit_bytes=40 * 2**20),
    )(w, gall)


def solution(mesh):
    return jax.shard_map(
        body,
        mesh=mesh,
        in_specs=(P("band", "grid", None, None), P("grid", None, None)),
        out_specs=P("band", "grid", None, None),
        check_vma=False,
    )
```
